512 devices in a mesh: ctx: 64 (over z, y_hi, core), exp: 8 (over x, y_lo).
Axes of the slice: x: 4, y: 8 (y_hi: 4, y_lo: 2; y = y_hi * 2 + y_lo), z: 8, core: 2. Of those that a mesh axis runs over, the one named last changes fastest.
Arguments:
- residual: bfloat16 [4096, 2048], P('ctx', 'exp'), may hold values from -60 to 60
- queries: bfloat16 [4096, 2048], P('ctx', 'exp'), may hold values from -6.5 to 6.5
- keys: bfloat16 [4096, 2048], P('ctx', 'exp'), may hold values from -6.5 to 6.5
- values: bfloat16 [4096, 2048], P('ctx', 'exp'), may hold values from -6 to 6
- out_proj: bfloat16 [2048, 2048], P(None, 'exp'), may hold values from -0.5 to 0.5
- norm_gain: float32 [2048], replicated, may hold values from 0.1 to 1.9
- w_gate: bfloat16 [8, 2048, 8192], P('exp', None, 'ctx'), may hold values from -0.125 to 0.125
- w_up: bfloat16 [8, 2048, 8192], P('exp', None, 'ctx'), may hold values from -0.125 to 0.125
- w_down: bfloat16 [8, 8192, 2048], P('exp', 'ctx'), may hold values from -0.0625 to 0.0625
- routes: int32 [4096, 1], P('ctx'), may hold values from 0 to 7; in each aligned block of 64 rows (0 to 63, 64 to 127, ...) at most 8 rows name the same one
- block_mask: int32 [32, 32], replicated, may hold values from 0 to 1, as said below
Outputs:
- mixed: bfloat16 [8, 512, 2048], P('exp', 'ctx')
The draws below stay inside these ranges and needn't reach their ends.
Inputs may be any that keep to these rules, and one draw needn't show every extreme that they name: `routes`: each stored row is named by exactly 8 of the 64 rows of one index of ctx. `block_mask`: every diagonal entry is 1.
All inputs are finite; a program needn't handle non-finite values.
Results may differ from the reference program's by a relative error of at most 0.006.
Values may be sent and summed in bfloat16 or wider, within the bound.
A program may use at most 64 MiB of HBM per device.

```python
import math
import jax
import jax.numpy as jnp
import numpy as np
from jax import lax

D = 2048
FF = 8192
HD = 128
BLK = 128
TOK_DEV = 64
S = 4096
HEADS = 16
EXPERTS = 8
NB = 32


def draw_queries(key, part):
    drawn = jnp.clip(1.3 * jax.random.normal(jax.random.fold_in(key, 11), (S, HEADS * HD), dtype=jnp.float32), -6.4, 6.4)
    return drawn.astype(jnp.bfloat16)


def draw_keys(key, part):
    drawn = jnp.clip(1.3 * jax.random.normal(jax.random.fold_in(key, 12), (S, HEADS * HD), dtype=jnp.float32), -6.4, 6.4)
    return drawn.astype(jnp.bfloat16)


def draw_residual(key, part):
    row_scale = jnp.exp(jax.random.uniform(jax.random.fold_in(key, 21), (S, 1), minval=-1.204, maxval=1.0986))
    col_scale = jnp.exp(jax.random.uniform(jax.random.fold_in(key, 22), (1, D), minval=-0.6931, maxval=1.6094))
    core = jnp.clip(jax.random.normal(jax.random.fold_in(key, 23), (S, D), dtype=jnp.float32), -4.0, 4.0)
    return (core * row_scale * col_scale).astype(jnp.bfloat16)


def draw_block_mask(key, part):
    modality = jax.random.randint(jax.random.fold_in(key, 31), (NB,), 0, 3)
    coin_flip = jax.random.randint(jax.random.fold_in(key, 32), (NB, NB), 0, 4)
    same_kind = modality[:, None] == modality[None, :]
    diagonal = jnp.arange(NB)[:, None] == jnp.arange(NB)[None, :]
    return jnp.where(same_kind | (coin_flip == 0) | diagonal, 1, 0).astype(jnp.int32)


def block_levels(own_key, extent, shards, least, largest):
    gain, own = 1.0, jax.random.fold_in(own_key, 6)
    for dim, blocks in shards:
        draws = jnp.exp(jax.random.uniform(jax.random.fold_in(own, dim), (blocks,), jnp.float32, least / len(shards), largest / len(shards)))
        gain = gain * jnp.repeat(draws, extent[dim] // blocks).reshape([-1 if axis == dim else 1 for axis in range(len(extent))])
    return gain


def deal_out(rng, own, number, rows, number_of, top, most, skew):
    order = jax.random.permutation(rng, number_of)
    crowded, ordinary = load_shares(number_of, rows * top, most, skew, True), load_shares(number_of, rows * top, most, skew, False)
    places = jnp.arange(number_of)

    def named(lengths, offset_by):
        used = int((lengths > 0).sum())
        fixed = max(1, used // 4)
        moved = fixed + (places - fixed + offset_by * (used - fixed)) % max(1, number_of - fixed)
        return jnp.zeros((number_of,), jnp.int32).at[order[jnp.where(places < fixed, places, moved)]].set(jnp.asarray(lengths, jnp.int32))

    lengths = jnp.where(number % 4 == 0, named(crowded, number // 4), named(ordinary, number - number // 4 - 1))
    mixed = jax.random.permutation(jax.random.fold_in(own, 3), number_of)
    source_of, taker = mixed[0:number_of // 2 * 2:2], mixed[1:number_of // 2 * 2:2]
    margin = jnp.minimum(lengths[source_of] - 1, most - lengths[taker]) // 2
    margin = jnp.where((source_of == order[0]) | (taker == order[0]) | (lengths[taker] == 0), 0, jnp.maximum(margin, 0))
    moved = jax.random.randint(jax.random.fold_in(own, 4), (number_of // 2,), 0, 1 << 20) % (margin + 1)
    lengths = lengths.at[source_of].add(-moved).at[taker].add(moved)
    items = jnp.searchsorted(jnp.cumsum(lengths), jnp.arange(rows * top), side="right").astype(jnp.int32)
    table = items.reshape(top, rows).T
    table = table[jax.random.permutation(jax.random.fold_in(own, 1), rows)]
    offset_by = jax.random.randint(jax.random.fold_in(own, 2), (rows, 1), 0, top)
    return jnp.take_along_axis(table, (jnp.arange(top)[None, :] + offset_by) % top, axis=1)


def load_shares(amount, total, reach, slope, full):
    loads = [(1 << 20) // math.isqrt(rank ** slope) + 1 for rank in range(1, amount + 1)]
    largest = reach if full else min(reach, max(-(-total // amount), total * loads[0] // sum(loads)))
    least = 1 if total - largest >= amount - 1 else 0
    counts, spare = [largest] + [least] * (amount - 1), total - largest - least * (amount - 1)
    while spare > 0:
        free = [i for i in range(1, amount) if counts[i] < largest] or [i for i in range(1, amount) if counts[i] < reach]
        whole, left = sum([loads[i] for i in free]), spare
        for i in free:
            more = min(reach - counts[i], max(1, left * loads[i] // whole), spare)
            counts[i] = counts[i] + more
            spare = spare - more
    return np.array(counts)


def centred(stream_key, dims, deviation, reach, shards=(), kind=jnp.bfloat16):
    entries = deviation * jax.random.normal(stream_key, dims, jnp.float32)
    if shards:
        entries = entries * block_levels(stream_key, dims, shards, -0.22, 0.18)
    return jnp.clip(entries, -reach, reach).astype(kind)


def setup_inputs(seed: int = 0) -> dict:
    key_of = jax.random.split(jax.random.key(seed), 12)
    residual = draw_residual(jax.random.fold_in(key_of[11], 71), 0)
    queries = draw_queries(jax.random.fold_in(key_of[11], 71), 0)
    keys = draw_keys(jax.random.fold_in(key_of[11], 71), 0)
    values = centred(key_of[3], (S, HEADS * HD), 1.0, 6.0, ((0, 64), (1, 8)))
    out_proj = centred(key_of[4], (HEADS * HD, D), HD ** -0.5, 0.5, ((1, 8),))
    norm_gain = jnp.clip(1.0 + 0.18 * jax.random.normal(key_of[5], (D,), jnp.float32), 0.1, 1.9)
    w_gate = centred(key_of[6], (EXPERTS, D, FF), D ** -0.5, 0.125, ((0, 8), (2, 64)))
    w_up = centred(key_of[7], (EXPERTS, D, FF), D ** -0.5, 0.125, ((0, 8), (2, 64)))
    w_down = centred(key_of[8], (EXPERTS, FF, D), FF ** -0.5, 0.0625, ((0, 8), (1, 64)))
    routes_keys = jax.random.split(jax.random.fold_in(key_of[9], 1), S // TOK_DEV)
    routes_turns = jax.random.permutation(jax.random.fold_in(key_of[9], 3), S // TOK_DEV)
    routes = jax.vmap(lambda own, number: deal_out(jax.random.fold_in(key_of[9], 2), own, number, TOK_DEV, EXPERTS, 1, TOK_DEV // EXPERTS, 0))(routes_keys, routes_turns).reshape((S, 1))
    block_mask = draw_block_mask(jax.random.fold_in(key_of[11], 71), 0)
    return dict(residual=residual, queries=queries, keys=keys, values=values, out_proj=out_proj, norm_gain=norm_gain, w_gate=w_gate, w_up=w_up, w_down=w_down, routes=routes, block_mask=block_mask)


def reference(residual, queries, keys, values, out_proj, norm_gain, w_gate, w_up, w_down, routes, block_mask):
    scaling = 1.0 / HD ** 0.5
    allowed = jnp.repeat(jnp.repeat(block_mask, BLK, axis=0), BLK, axis=1) > 0
    query_heads = queries.reshape(S, HEADS, HD).transpose(1, 0, 2)
    key_heads = keys.reshape(S, HEADS, HD).transpose(1, 0, 2)
    value_heads = values.reshape(S, HEADS, HD).transpose(1, 0, 2)

    def one_head(triple):
        query_h, key_h, value_h = triple
        scores = jnp.dot(query_h, key_h.T, preferred_element_type=jnp.float32) * scaling
        scores = jnp.where(allowed, scores, -1e+30)
        top_row = lax.optimization_barrier(jnp.max(scores, axis=1, keepdims=True))
        exponent = jnp.where(allowed, jnp.exp(scores - top_row), 0.0)
        totals = lax.optimization_barrier(jnp.sum(exponent, axis=1, keepdims=True))
        weights = exponent.astype(jnp.bfloat16)
        summed_v = jnp.dot(weights, value_h, preferred_element_type=jnp.float32)
        return (summed_v / totals).astype(jnp.bfloat16)
    attended = lax.map(one_head, (query_heads, key_heads, value_heads))
    attended = attended.transpose(1, 0, 2).reshape(S, HEADS * HD)
    hidden = (residual.astype(jnp.float32) + jnp.dot(attended, out_proj, preferred_element_type=jnp.float32)).astype(jnp.bfloat16)
    hidden_f = hidden.astype(jnp.float32)
    meansq = lax.optimization_barrier(jnp.mean(hidden_f * hidden_f, axis=1, keepdims=True))
    normed = (hidden_f * lax.rsqrt(meansq + 1e-05) * norm_gain).astype(jnp.bfloat16)
    position = jnp.arange(S, dtype=jnp.int32)
    target = routes[:, 0].astype(jnp.int32)
    order = jnp.argsort(target * S + position)
    chosen = order.reshape(EXPERTS, S // EXPERTS)

    def one_expert(bundle):
        picked, gate_w, up_w, down_w = bundle
        inputs = normed[picked]
        gate_v = jnp.dot(inputs, gate_w, preferred_element_type=jnp.float32)
        up_v = jnp.dot(inputs, up_w, preferred_element_type=jnp.float32)
        activ = (jax.nn.silu(gate_v) * up_v).astype(jnp.bfloat16)
        output = jnp.dot(activ, down_w, preferred_element_type=jnp.float32)
        return (hidden_f[picked] + output).astype(jnp.bfloat16)
    return lax.map(one_expert, (chosen, w_gate, w_up, w_down))
```

```python
import functools
import math

import jax
import jax.numpy as jnp
from jax import lax
from jax.experimental import pallas as pl
from jax.experimental.pallas import tpu as pltpu
from jax.sharding import PartitionSpec as P

HD = 128
BLK = 128
ROWS_Y = 4
ANY = pl.BlockSpec(memory_space=pl.ANY)
VM = pl.BlockSpec(memory_space=pltpu.VMEM)
MESH = pl.DeviceIdType.MESH
DMA = pltpu.SemaphoreType.DMA


def place(ny):
    me = lax.axis_index("ctx")
    return lax.div(me, 2 * ny), lax.rem(lax.div(me, 2), ny), lax.rem(me, 2)


def greet(peers):
    barrier = pltpu.get_barrier_semaphore()
    for peer in peers:
        pl.semaphore_signal(barrier, inc=1, device_id=peer, device_id_type=MESH)
    pl.semaphore_wait(barrier, len(peers))


def remote(src, dst, send, recv, peer):
    return pltpu.make_async_remote_copy(
        src_ref=src, dst_ref=dst, send_sem=send, recv_sem=recv, device_id=peer, device_id_type=MESH
    )


def spread(nz, ny, at, peer, block, forward):
    z, y, c = at
    y_send, y_recv, f_send, f_recv, b_send, b_recv = block["sems"]
    ref = block["ref"]
    up, down = lax.rem(z + 1, nz), lax.rem(z + nz - 1, nz)
    pending = []

    def go(copy):
        copy.start()
        pending.append(copy)

    for dy in range(1, ny):
        go(remote(ref(z, y), ref(z, y), y_send.at[dy], y_recv.at[dy], peer(z, lax.rem(y + dy, ny), c)))
    half = nz // 2
    events = [(s + j, j, s, d) for j in range(ny) for s in range(half + 1) for d in (1, -1)]
    for _, j, s, d in sorted(events, key=lambda e: (e[0], e[1], e[2], -e[3])):
        yy = lax.rem(y + ny - j, ny)
        longer = 1 if j % 2 == 0 else -1
        hops = half if d == longer else half - 1
        if s > hops or (s == 0 and d == -1):
            continue
        send, recv = (f_send, f_recv) if d == 1 else (b_send, b_recv)
        zz = lax.rem(z + nz - d * s, nz)
        here = ref(zz, yy)
        if s == 0:
            if j > 0:
                remote(here, here, y_send.at[j], y_recv.at[j], peer(z, yy, c)).wait_recv()
            for d0 in (1, -1):
                hops0 = half if d0 == longer else half - 1
                s0, r0 = (f_send, f_recv) if d0 == 1 else (b_send, b_recv)
                if hops0 > 0:
                    go(remote(here, here, s0.at[j, 0], r0.at[j, 0], peer(up if d0 == 1 else down, y, c)))
        else:
            remote(here, here, send.at[j, s - 1], recv.at[j, s - 1], peer(down if d == 1 else up, y, c)).wait_recv()
            if s < hops:
                go(remote(here, here, send.at[j, s], recv.at[j, s], peer(up if d == 1 else down, y, c)))
        forward(zz, yy, j, s if d == 1 else nz - s)
    return pending


def ctx_peer(ny):
    return lambda z, y, c: {"ctx": (z * ny + y) * 2 + c}


def ring_peers(nz, ny, at, peer):
    z, y, c = at
    out = [peer(z, y, 1 - c)]
    out += [peer(z, lax.rem(y + dy, ny), c) for dy in range(1, ny)]
    out += [peer(lax.rem(z + 1, nz), y, c), peer(lax.rem(z + nz - 1, nz), y, c)]
    return out


def keys_kernel(nz, ny, q_ref, kv_ref, qo_ref, g_ref, own, d_send, d_recv, *sems):
    at = z, y, c = place(ny)
    peer = ctx_peer(ny)
    greet(ring_peers(nz, ny, at, peer))
    other = peer(z, y, 1 - c)
    swap_kv = remote(kv_ref.at[1 - c], g_ref.at[z, y, c], d_send.at[0], d_recv.at[0], other)
    swap_q = remote(q_ref.at[1 - c], qo_ref.at[c], d_send.at[1], d_recv.at[1], other)
    swap_kv.start()
    swap_q.start()
    keep_kv = pltpu.make_async_copy(kv_ref.at[c], g_ref.at[z, y, c], own.at[0])
    keep_q = pltpu.make_async_copy(q_ref.at[c], qo_ref.at[c], own.at[1])
    keep_kv.start()
    keep_q.start()
    keep_kv.wait()
    got = g_ref.at[z, y, 1 - c]
    remote(got, got, d_send.at[0], d_recv.at[0], other).wait_recv()
    block = {"ref": lambda zz, yy: g_ref.at[zz, yy], "sems": sems}
    pending = spread(nz, ny, at, peer, block, lambda *a: None)
    for copy in pending:
        copy.wait_send()
    keep_q.wait()
    got_q = qo_ref.at[1 - c]
    remote(got_q, got_q, d_send.at[1], d_recv.at[1], other).wait_recv()
    swap_kv.wait_send()
    swap_q.wait_send()


def rows_kernel(nz, ny, x_ref, g_ref, own, d_send, d_recv, *sems):
    at = z, y, c = place(ny)
    peer = ctx_peer(ny)
    keep = pltpu.make_async_copy(x_ref, g_ref.at[z, y, c], own)
    keep.start()
    greet(ring_peers(nz, ny, at, peer))
    keep.wait()
    other = peer(z, y, 1 - c)
    passed = []

    def forward(zz, yy, j, s):
        here = g_ref.at[zz, yy, c]
        copy = remote(here, here, d_send.at[j, s], d_recv.at[j, s], other)
        copy.start()
        passed.append((copy, zz, yy, j, s))

    block = {"ref": lambda zz, yy: g_ref.at[zz, yy, c], "sems": sems}
    pending = spread(nz, ny, at, peer, block, forward)
    for copy, zz, yy, j, s in passed:
        got = g_ref.at[zz, yy, 1 - c]
        remote(got, got, d_send.at[j, s], d_recv.at[j, s], other).wait_recv()
    for copy, *_ in passed:
        copy.wait_send()
    for copy in pending:
        copy.wait_send()


def ring_sems(nz, ny):
    return [DMA((ny,))] * 2 + [DMA((ny, nz))] * 4


def gather_keys(q2, kv2, nz, ny):
    return pl.pallas_call(
        functools.partial(keys_kernel, nz, ny),
        out_shape=(
            jax.ShapeDtypeStruct(q2.shape, q2.dtype),
            jax.ShapeDtypeStruct((nz, ny) + kv2.shape, kv2.dtype),
        ),
        in_specs=[VM, VM],
        out_specs=(VM, VM),
        scratch_shapes=[DMA((2,)), DMA((2,)), DMA((2,))] + ring_sems(nz, ny),
        compiler_params=pltpu.CompilerParams(collective_id=0, has_side_effects=True),
    )(q2, kv2)


def gather_rows(x, nz, ny):
    return pl.pallas_call(
        functools.partial(rows_kernel, nz, ny),
        out_shape=jax.ShapeDtypeStruct((nz, ny, 2) + x.shape, x.dtype),
        in_specs=[VM],
        out_specs=VM,
        scratch_shapes=[DMA, DMA((ny, nz)), DMA((ny, nz))] + ring_sems(nz, ny),
        compiler_params=pltpu.CompilerParams(collective_id=1, has_side_effects=True),
    )(x)


def heads_kernel(ny, ne, a_ref, o_ref, own, send, recv):
    z, y, c = place(ny)
    e = lax.axis_index("exp")

    def peer(de, dc):
        return {
            "ctx": (z * ny + y) * 2 + lax.rem(c + dc, 2),
            "exp": lax.rem(e + de, ne),
        }

    others = [(de, dc) for de in range(ne) for dc in range(2) if de or dc]
    keep = pltpu.make_async_copy(a_ref.at[c], o_ref.at[e, c], own)
    keep.start()
    greet([peer(de, dc) for de, dc in others])
    copies = []
    for de, dc in others:
        copy = remote(
            a_ref.at[lax.rem(c + dc, 2)], o_ref.at[e, c], send.at[de, dc], recv.at[de, dc], peer(de, dc)
        )
        copy.start()
        copies.append(copy)
    keep.wait()
    for de, dc in others:
        got = o_ref.at[lax.rem(e + ne - de, ne), lax.rem(c + dc, 2)]
        remote(got, got, send.at[de, dc], recv.at[de, dc], peer(de, dc)).wait_recv()
    for copy in copies:
        copy.wait_send()


def share_heads(a, ny, ne):
    return pl.pallas_call(
        functools.partial(heads_kernel, ny, ne),
        out_shape=jax.ShapeDtypeStruct((ne,) + a.shape, a.dtype),
        in_specs=[VM],
        out_specs=VM,
        scratch_shapes=[DMA, DMA((ne, 2)), DMA((ne, 2))],
        compiler_params=pltpu.CompilerParams(collective_id=2, has_side_effects=True),
    )(a)


def sum_kernel(nz, ny, t_ref, h_ref, o_ref, d_buf, s_buf, r_buf, u_buf, v_buf, d_send, d_recv,
               z_send, z_recv, y_send, y_recv):
    z, y, c = place(ny)
    peer = ctx_peer(ny)
    other = peer(z, y, 1 - c)
    peers = [other]
    peers += [peer(lax.rem(z + dz, nz), y, c) for dz in range(1, nz)]
    peers += [peer(z, lax.rem(y + dy, ny), c) for dy in range(1, ny)]
    greet(peers)
    order = sorted(range(1, nz), key=lambda d: -min(d, nz - d)) + [0]
    halves = []
    for dz in order:
        zz = lax.rem(z + dz, nz)
        copy = remote(t_ref.at[zz, :, 1 - c], d_buf.at[dz], d_send.at[dz], d_recv.at[dz], other)
        copy.start()
        halves.append(copy)
    sent = []
    for dz, half in zip(order, halves):
        zz = lax.rem(z + dz, nz)
        half.wait_recv()
        both = t_ref[zz, :, c].astype(jnp.float32) + d_buf[dz].astype(jnp.float32)
        if dz == 0:
            total = both
        else:
            s_buf[dz] = both.astype(jnp.bfloat16)
            copy = remote(s_buf.at[dz], r_buf.at[dz], z_send.at[dz], z_recv.at[dz], peer(zz, y, c))
            copy.start()
            sent.append(copy)
    for copy, dz in zip(sent, order):
        copy.wait_recv()
        total = total + r_buf[dz].astype(jnp.float32)
    u_buf[...] = total.astype(jnp.bfloat16)
    across = []
    for dy in range(1, ny):
        yy = lax.rem(y + dy, ny)
        copy = remote(u_buf.at[yy], v_buf.at[dy], y_send.at[dy], y_recv.at[dy], peer(z, yy, c))
        copy.start()
        across.append(copy)
    result = u_buf[y].astype(jnp.float32)
    for dy, copy in zip(range(1, ny), across):
        copy.wait_recv()
        result = result + v_buf[dy].astype(jnp.float32)
    o_ref[...] = (h_ref[...].astype(jnp.float32) + result).astype(jnp.bfloat16)
    for copy in halves + sent + across:
        copy.wait_send()


def sum_rows(terms, own, nz, ny):
    rows, width = own.shape
    t = terms.reshape(nz, ny, 2, rows, width)
    big = pltpu.VMEM((nz, ny, rows, width), jnp.bfloat16)
    small = pltpu.VMEM((ny, rows, width), jnp.bfloat16)
    return pl.pallas_call(
        functools.partial(sum_kernel, nz, ny),
        out_shape=jax.ShapeDtypeStruct(own.shape, own.dtype),
        in_specs=[VM, VM],
        out_specs=VM,
        scratch_shapes=[big, big, big, small, small, DMA((nz,)), DMA((nz,)), DMA((nz,)), DMA((nz,)),
                        DMA((ny,)), DMA((ny,))],
        compiler_params=pltpu.CompilerParams(collective_id=3, has_side_effects=True),
    )(t, own)


def body(
    residual, queries, keys, values, out_proj, norm_gain, w_gate, w_up, w_down, routes, block_mask
):
    local_tokens = residual.shape[0]
    blocks_all = block_mask.shape[0]
    expert_count = lax.axis_size("exp")
    ny = ROWS_Y
    nz = lax.axis_size("ctx") // (2 * ny)
    per_expert = local_tokens // expert_count
    scaling = 1.0 / math.sqrt(HD)
    ctx_place = lax.axis_index("ctx")
    q2 = queries.reshape(local_tokens, 2, HD).transpose(1, 0, 2)
    kv2 = jnp.concatenate(
        [
            keys.reshape(local_tokens, 2, HD).transpose(1, 0, 2),
            values.reshape(local_tokens, 2, HD).transpose(1, 0, 2),
        ],
        axis=2,
    )
    q_chip, kv_all = gather_keys(q2, kv2, nz, ny)
    chip_tokens = 2 * local_tokens
    q_chip = q_chip.reshape(chip_tokens, HD)
    kv_all = kv_all.reshape(-1, 2 * HD)
    count = kv_all.shape[0]
    query_pos = (ctx_place // 2) * chip_tokens + jnp.arange(chip_tokens, dtype=jnp.int32)
    query_blocks = jax.nn.one_hot(query_pos // BLK, blocks_all, dtype=jnp.float32)
    query_mask = jnp.dot(query_blocks, block_mask.astype(jnp.float32))
    key_pos = jnp.arange(count, dtype=jnp.int32)
    key_blocks = jax.nn.one_hot(key_pos // BLK, blocks_all, dtype=jnp.float32)
    allowed = jnp.dot(query_mask, key_blocks.T) > 0.5
    scores = (
        jnp.einsum("qd,kd->qk", q_chip, kv_all[:, :HD], preferred_element_type=jnp.float32) * scaling
    )
    scores = jnp.where(allowed, scores, -1e30)
    top = jnp.max(scores, axis=1, keepdims=True)
    exponent = jnp.where(allowed, jnp.exp(scores - top), 0.0)
    total = jnp.sum(exponent, axis=1, keepdims=True)
    product = jnp.dot(
        exponent.astype(jnp.bfloat16), kv_all[:, HD:], preferred_element_type=jnp.float32
    )
    attended = (product / total).astype(jnp.bfloat16).reshape(2, local_tokens, HD)
    heads = share_heads(attended, ny, expert_count)
    heads = heads.reshape(2 * expert_count, local_tokens, HD)
    heads = heads.transpose(1, 0, 2).reshape(local_tokens, 2 * expert_count * HD)
    projected = jnp.dot(heads, out_proj, preferred_element_type=jnp.float32)
    hidden = (residual.astype(jnp.float32) + projected).astype(jnp.bfloat16)
    target = routes[:, 0]
    token_ids = jnp.arange(local_tokens, dtype=jnp.int32)
    earlier = (target[:, None] == target[None, :]) & (token_ids[None, :] < token_ids[:, None])
    ranking = jnp.sum(earlier.astype(jnp.int32), axis=1)
    slot_of = target * per_expert + ranking
    slot_ids = jnp.arange(expert_count * per_expert, dtype=jnp.int32)
    placing = (slot_of[None, :] == slot_ids[:, None]).astype(jnp.bfloat16)
    send_buffer = jnp.dot(placing, hidden, preferred_element_type=jnp.float32).astype(jnp.bfloat16)
    send_buffer = send_buffer.reshape(expert_count, per_expert, hidden.shape[1])
    own_rows = lax.all_to_all(send_buffer, "exp", split_axis=0, concat_axis=2, tiled=True)[0]
    values_f = own_rows.astype(jnp.float32)
    meansq = jnp.mean(values_f * values_f, axis=1, keepdims=True)
    normed_own = (values_f * lax.rsqrt(meansq + 1e-05) * norm_gain).astype(jnp.bfloat16)
    normed_rows = gather_rows(normed_own, nz, ny).reshape(-1, normed_own.shape[1])
    gate_v = jnp.dot(normed_rows, w_gate[0], preferred_element_type=jnp.float32)
    up_v = jnp.dot(normed_rows, w_up[0], preferred_element_type=jnp.float32)
    activ = (jax.nn.silu(gate_v) * up_v).astype(jnp.bfloat16)
    terms = jnp.dot(activ, w_down[0], preferred_element_type=jnp.float32).astype(jnp.bfloat16)
    return sum_rows(terms, own_rows, nz, ny)[None]


def solution(mesh):
    in_specs = (
        P("ctx", "exp"),
        P("ctx", "exp"),
        P("ctx", "exp"),
        P("ctx", "exp"),
        P(None, "exp"),
        P(),
        P("exp", None, "ctx"),
        P("exp", None, "ctx"),
        P("exp", "ctx", None),
        P("ctx", None),
        P(),
    )
    out_specs = P("exp", "ctx", None)
    return jax.shard_map(body, mesh=mesh, in_specs=in_specs, out_specs=out_specs, check_vma=False)
```

```python
import functools
import math

import jax
import jax.numpy as jnp
from jax import lax
from jax.experimental import pallas as pl
from jax.experimental.pallas import tpu as pltpu
from jax.sharding import PartitionSpec as P

HD = 128
BLK = 128
ROWS_Y = 4
ANY = pl.BlockSpec(memory_space=pl.ANY)
VM = pl.BlockSpec(memory_space=pltpu.VMEM)
MESH = pl.DeviceIdType.MESH
DMA = pltpu.SemaphoreType.DMA


def place(ny):
    me = lax.axis_index("ctx")
    return lax.div(me, 2 * ny), lax.rem(lax.div(me, 2), ny), lax.rem(me, 2)


def greet(peers):
    barrier = pltpu.get_barrier_semaphore()
    for peer in peers:
        pl.semaphore_signal(barrier, inc=1, device_id=peer, device_id_type=MESH)
    pl.semaphore_wait(barrier, len(peers))


def remote(src, dst, send, recv, peer):
    return pltpu.make_async_remote_copy(
        src_ref=src, dst_ref=dst, send_sem=send, recv_sem=recv, device_id=peer, device_id_type=MESH
    )


def spread(nz, ny, at, peer, ref, sems):
    z, y, c = at
    y_send, y_recv, f_send, f_recv, b_send, b_recv = sems
    up, down = lax.rem(z + 1, nz), lax.rem(z + nz - 1, nz)
    pending = []

    def go(copy):
        copy.start()
        pending.append(copy)

    for dy in range(1, ny):
        go(remote(ref(z, y), ref(z, y), y_send.at[dy], y_recv.at[dy], peer(z, lax.rem(y + dy, ny), c)))
    half = nz // 2
    events = [(s + j, j, s, d) for j in range(ny) for s in range(half + 1) for d in (1, -1)]
    for _, j, s, d in sorted(events, key=lambda e: (e[0], e[1], e[2], -e[3])):
        yy = lax.rem(y + ny - j, ny)
        longer = 1 if j % 2 == 0 else -1
        hops = half if d == longer else half - 1
        if s > hops or (s == 0 and d == -1):
            continue
        send, recv = (f_send, f_recv) if d == 1 else (b_send, b_recv)
        zz = lax.rem(z + nz - d * s, nz)
        here = ref(zz, yy)
        if s == 0:
            if j > 0:
                remote(here, here, y_send.at[j], y_recv.at[j], peer(z, yy, c)).wait_recv()
            for d0 in (1, -1):
                hops0 = half if d0 == longer else half - 1
                s0, r0 = (f_send, f_recv) if d0 == 1 else (b_send, b_recv)
                if hops0 > 0:
                    go(remote(here, here, s0.at[j, 0], r0.at[j, 0], peer(up if d0 == 1 else down, y, c)))
        else:
            remote(here, here, send.at[j, s - 1], recv.at[j, s - 1], peer(down if d == 1 else up, y, c)).wait_recv()
            if s < hops:
                go(remote(here, here, send.at[j, s], recv.at[j, s], peer(up if d == 1 else down, y, c)))
    return pending


def ctx_peer(ny):
    return lambda z, y, c: {"ctx": (z * ny + y) * 2 + c}


def ring_peers(nz, ny, at, peer):
    z, y, c = at
    out = [peer(z, lax.rem(y + dy, ny), c) for dy in range(1, ny)]
    out += [peer(lax.rem(z + 1, nz), y, c), peer(lax.rem(z + nz - 1, nz), y, c)]
    return out


def keys_kernel(
    nz, ny, q_ref, kv_ref, w0, w1, w2, qo_ref, g_ref, p0, p1, p2, own, d_send, d_recv, *sems
):
    at = z, y, c = place(ny)
    peer = ctx_peer(ny)
    other = peer(z, y, 1 - c)
    greet(ring_peers(nz, ny, at, peer) + [other])
    swap_kv = remote(kv_ref.at[1 - c], g_ref.at[z, y, c], d_send.at[0], d_recv.at[0], other)
    swap_q = remote(q_ref.at[1 - c], qo_ref.at[c], d_send.at[1], d_recv.at[1], other)
    swap_kv.start()
    swap_q.start()
    keep_kv = pltpu.make_async_copy(kv_ref.at[c], g_ref.at[z, y, c], own.at[0])
    keep_q = pltpu.make_async_copy(q_ref.at[c], qo_ref.at[c], own.at[1])
    keep_kv.start()
    keep_q.start()
    keep_kv.wait()
    got = g_ref.at[z, y, 1 - c]
    remote(got, got, d_send.at[0], d_recv.at[0], other).wait_recv()
    weights = [
        remote(src, dst, d_send.at[2 + i], d_recv.at[2 + i], other)
        for i, (src, dst) in enumerate([(w0, p0), (w1, p1), (w2, p2)])
    ]
    for copy in weights:
        copy.start()
    pending = spread(nz, ny, at, peer, lambda zz, yy: g_ref.at[zz, yy], sems)
    for copy in pending:
        copy.wait_send()
    for copy in weights:
        copy.wait()
    keep_q.wait()
    got_q = qo_ref.at[1 - c]
    remote(got_q, got_q, d_send.at[1], d_recv.at[1], other).wait_recv()
    swap_kv.wait_send()
    swap_q.wait_send()


def rows_kernel(nz, ny, x_ref, g_ref, own, *sems):
    at = z, y, c = place(ny)
    peer = ctx_peer(ny)
    keep = pltpu.make_async_copy(x_ref, g_ref.at[z, y], own)
    keep.start()
    greet(ring_peers(nz, ny, at, peer))
    keep.wait()
    for copy in spread(nz, ny, at, peer, lambda zz, yy: g_ref.at[zz, yy], sems):
        copy.wait_send()


def ring_sems(nz, ny):
    return [DMA((ny,))] * 2 + [DMA((ny, nz))] * 4


def gather_keys(q2, kv2, weights, nz, ny):
    return pl.pallas_call(
        functools.partial(keys_kernel, nz, ny),
        out_shape=(
            jax.ShapeDtypeStruct(q2.shape, q2.dtype),
            jax.ShapeDtypeStruct((nz, ny) + kv2.shape, kv2.dtype),
            *(jax.ShapeDtypeStruct(w.shape, w.dtype) for w in weights),
        ),
        in_specs=[VM, VM, ANY, ANY, ANY],
        out_specs=(VM, VM, ANY, ANY, ANY),
        scratch_shapes=[DMA((2,)), DMA((5,)), DMA((5,))] + ring_sems(nz, ny),
        compiler_params=pltpu.CompilerParams(collective_id=0, has_side_effects=True),
    )(q2, kv2, *weights)


def gather_rows(x, nz, ny):
    return pl.pallas_call(
        functools.partial(rows_kernel, nz, ny),
        out_shape=jax.ShapeDtypeStruct((nz, ny) + x.shape, x.dtype),
        in_specs=[VM],
        out_specs=VM,
        scratch_shapes=[DMA] + ring_sems(nz, ny),
        compiler_params=pltpu.CompilerParams(collective_id=1, has_side_effects=True),
    )(x)


def heads_kernel(ny, ne, a_ref, o_ref, own, send, recv):
    z, y, c = place(ny)
    e = lax.axis_index("exp")

    def peer(de, dc):
        return {
            "ctx": (z * ny + y) * 2 + lax.rem(c + dc, 2),
            "exp": lax.rem(e + de, ne),
        }

    others = [(de, dc) for de in range(ne) for dc in range(2) if de or dc]
    keep = pltpu.make_async_copy(a_ref.at[c], o_ref.at[e, c], own)
    keep.start()
    greet([peer(de, dc) for de, dc in others])
    copies = []
    for de, dc in others:
        copy = remote(
            a_ref.at[lax.rem(c + dc, 2)], o_ref.at[e, c], send.at[de, dc], recv.at[de, dc], peer(de, dc)
        )
        copy.start()
        copies.append(copy)
    keep.wait()
    for de, dc in others:
        got = o_ref.at[lax.rem(e + ne - de, ne), lax.rem(c + dc, 2)]
        remote(got, got, send.at[de, dc], recv.at[de, dc], peer(de, dc)).wait_recv()
    for copy in copies:
        copy.wait_send()


def share_heads(a, ny, ne):
    return pl.pallas_call(
        functools.partial(heads_kernel, ny, ne),
        out_shape=jax.ShapeDtypeStruct((ne,) + a.shape, a.dtype),
        in_specs=[VM],
        out_specs=VM,
        scratch_shapes=[DMA, DMA((ne, 2)), DMA((ne, 2))],
        compiler_params=pltpu.CompilerParams(collective_id=2, has_side_effects=True),
    )(a)


def pieces_kernel(ne, x_ref, o_ref, own, send, recv):
    e = lax.axis_index("exp")
    keep = pltpu.make_async_copy(x_ref.at[e], o_ref.at[e], own)
    keep.start()
    greet([{"exp": lax.rem(e + de, ne)} for de in range(1, ne)])
    copies = []
    for de in range(1, ne):
        to = lax.rem(e + de, ne)
        copy = remote(x_ref.at[to], o_ref.at[e], send.at[de], recv.at[de], {"exp": to})
        copy.start()
        copies.append(copy)
    keep.wait()
    for de in range(1, ne):
        back = lax.rem(e + ne - de, ne)
        got = o_ref.at[back]
        remote(got, got, send.at[de], recv.at[de], {"exp": back}).wait_recv()
    for copy in copies:
        copy.wait_send()


def share_pieces(x, ne):
    return pl.pallas_call(
        functools.partial(pieces_kernel, ne),
        out_shape=jax.ShapeDtypeStruct(x.shape, x.dtype),
        in_specs=[VM],
        out_specs=VM,
        scratch_shapes=[DMA, DMA((ne,)), DMA((ne,))],
        compiler_params=pltpu.CompilerParams(collective_id=4, has_side_effects=True),
    )(x)


def sum_kernel(nz, ny, t_ref, h_ref, o_ref, rz, ry, uz, uy, vz, vy, *sems):
    z, y, c = place(ny)
    rz_send, rz_recv, ry_send, ry_recv, vz_send, vz_recv, vy_send, vy_recv = sems
    half = t_ref.shape[-1] // 2
    left, right = pl.ds(0, half), pl.ds(half, half)
    peer = ctx_peer(ny)
    far_z = sorted(range(1, nz), key=lambda d: -min(d, nz - d))
    far_y = sorted(range(1, ny), key=lambda d: -min(d, ny - d))
    to_z = {d: lax.rem(z + d, nz) for d in far_z}
    to_y = {d: lax.rem(y + d, ny) for d in far_y}
    greet([peer(to_z[d], y, c) for d in far_z] + [peer(z, to_y[d], c) for d in far_y])

    def send(src, dst, sends, recvs, who):
        copy = remote(src, dst, sends, recvs, who)
        copy.start()
        return copy

    by_z = [
        send(t_ref.at[to_z[d], :, :, left], rz.at[d], rz_send.at[d], rz_recv.at[d], peer(to_z[d], y, c))
        for d in far_z
    ]
    by_y = [
        send(t_ref.at[:, to_y[d], :, right], ry.at[d], ry_send.at[d], ry_recv.at[d], peer(z, to_y[d], c))
        for d in far_y
    ]
    total = t_ref[z, :, :, :half].astype(jnp.float32)
    for d, copy in zip(far_z, by_z):
        copy.wait_recv()
        total = total + rz[d].astype(jnp.float32)
    uz[...] = total.astype(jnp.bfloat16)
    then_y = [
        send(uz.at[to_y[d]], vz.at[d], vz_send.at[d], vz_recv.at[d], peer(z, to_y[d], c)) for d in far_y
    ]
    total = t_ref[:, y, :, half:].astype(jnp.float32)
    for d, copy in zip(far_y, by_y):
        copy.wait_recv()
        total = total + ry[d].astype(jnp.float32)
    uy[...] = total.astype(jnp.bfloat16)
    then_z = [
        send(uy.at[to_z[d]], vy.at[d], vy_send.at[d], vy_recv.at[d], peer(to_z[d], y, c)) for d in far_z
    ]
    result = h_ref[:, :half].astype(jnp.float32) + uz[y].astype(jnp.float32)
    for d, copy in zip(far_y, then_y):
        copy.wait_recv()
        result = result + vz[d].astype(jnp.float32)
    o_ref[:, :half] = result.astype(jnp.bfloat16)
    result = h_ref[:, half:].astype(jnp.float32) + uy[z].astype(jnp.float32)
    for d, copy in zip(far_z, then_z):
        copy.wait_recv()
        result = result + vy[d].astype(jnp.float32)
    o_ref[:, half:] = result.astype(jnp.bfloat16)
    for copy in by_z + by_y + then_y + then_z:
        copy.wait_send()


def sum_rows(terms, own, nz, ny):
    rows, width = own.shape
    half = width // 2
    t = terms.reshape(nz, ny, rows, width)

    def buf(*lead):
        return pltpu.VMEM(lead + (rows, half), jnp.bfloat16)

    return pl.pallas_call(
        functools.partial(sum_kernel, nz, ny),
        out_shape=jax.ShapeDtypeStruct(own.shape, own.dtype),
        in_specs=[VM, VM],
        out_specs=VM,
        scratch_shapes=[buf(nz, ny), buf(ny, nz), buf(ny), buf(nz), buf(ny), buf(nz)]
        + [DMA((n,)) for n in (nz, nz, ny, ny, ny, ny, nz, nz)],
        compiler_params=pltpu.CompilerParams(collective_id=3, has_side_effects=True),
    )(t, own)


def body(
    residual, queries, keys, values, out_proj, norm_gain, w_gate, w_up, w_down, routes, block_mask
):
    local_tokens = residual.shape[0]
    blocks_all = block_mask.shape[0]
    expert_count = lax.axis_size("exp")
    ny = ROWS_Y
    nz = lax.axis_size("ctx") // (2 * ny)
    per_expert = local_tokens // expert_count
    scaling = 1.0 / math.sqrt(HD)
    ctx_place = lax.axis_index("ctx")
    q2 = queries.reshape(local_tokens, 2, HD).transpose(1, 0, 2)
    kv2 = jnp.concatenate(
        [
            keys.reshape(local_tokens, 2, HD).transpose(1, 0, 2),
            values.reshape(local_tokens, 2, HD).transpose(1, 0, 2),
        ],
        axis=2,
    )
    mine = (w_gate[0], w_up[0], w_down[0])
    q_chip, kv_all, *partner = gather_keys(q2, kv2, mine, nz, ny)
    chip_tokens = 2 * local_tokens
    q_chip = q_chip.reshape(chip_tokens, HD)
    kv_all = kv_all.reshape(-1, 2 * HD)
    count = kv_all.shape[0]
    query_pos = (ctx_place // 2) * chip_tokens + jnp.arange(chip_tokens, dtype=jnp.int32)
    query_blocks = jax.nn.one_hot(query_pos // BLK, blocks_all, dtype=jnp.float32)
    query_mask = jnp.dot(query_blocks, block_mask.astype(jnp.float32))
    key_pos = jnp.arange(count, dtype=jnp.int32)
    key_blocks = jax.nn.one_hot(key_pos // BLK, blocks_all, dtype=jnp.float32)
    allowed = jnp.dot(query_mask, key_blocks.T) > 0.5
    scores = (
        jnp.einsum("qd,kd->qk", q_chip, kv_all[:, :HD], preferred_element_type=jnp.float32) * scaling
    )
    scores = jnp.where(allowed, scores, -1e30)
    top = jnp.max(scores, axis=1, keepdims=True)
    exponent = jnp.where(allowed, jnp.exp(scores - top), 0.0)
    total = jnp.sum(exponent, axis=1, keepdims=True)
    product = jnp.dot(
        exponent.astype(jnp.bfloat16), kv_all[:, HD:], preferred_element_type=jnp.float32
    )
    attended = (product / total).astype(jnp.bfloat16).reshape(2, local_tokens, HD)
    heads = share_heads(attended, ny, expert_count)
    heads = heads.reshape(2 * expert_count, local_tokens, HD)
    heads = heads.transpose(1, 0, 2).reshape(local_tokens, 2 * expert_count * HD)
    projected = jnp.dot(heads, out_proj, preferred_element_type=jnp.float32)
    hidden = (residual.astype(jnp.float32) + projected).astype(jnp.bfloat16)
    target = routes[:, 0]
    token_ids = jnp.arange(local_tokens, dtype=jnp.int32)
    earlier = (target[:, None] == target[None, :]) & (token_ids[None, :] < token_ids[:, None])
    ranking = jnp.sum(earlier.astype(jnp.int32), axis=1)
    slot_of = target * per_expert + ranking
    slot_ids = jnp.arange(expert_count * per_expert, dtype=jnp.int32)
    placing = (slot_of[None, :] == slot_ids[:, None]).astype(jnp.bfloat16)
    send_buffer = jnp.dot(placing, hidden, preferred_element_type=jnp.float32).astype(jnp.bfloat16)
    send_buffer = send_buffer.reshape(expert_count, per_expert, hidden.shape[1])
    own_rows = share_pieces(send_buffer, expert_count).transpose(1, 0, 2).reshape(per_expert, -1)
    values_f = own_rows.astype(jnp.float32)
    meansq = jnp.mean(values_f * values_f, axis=1, keepdims=True)
    normed_own = (values_f * lax.rsqrt(meansq + 1e-05) * norm_gain).astype(jnp.bfloat16)
    normed_rows = gather_rows(normed_own, nz, ny).reshape(-1, normed_own.shape[1])
    terms = 0.0
    for gate, up, down in (mine, partner):
        gate_v = jnp.dot(normed_rows, gate, preferred_element_type=jnp.float32)
        up_v = jnp.dot(normed_rows, up, preferred_element_type=jnp.float32)
        activ = (jax.nn.silu(gate_v) * up_v).astype(jnp.bfloat16)
        terms = terms + jnp.dot(activ, down, preferred_element_type=jnp.float32)
    terms = terms.astype(jnp.bfloat16)
    return sum_rows(terms, own_rows, nz, ny)[None]


def solution(mesh):
    in_specs = (
        P("ctx", "exp"),
        P("ctx", "exp"),
        P("ctx", "exp"),
        P("ctx", "exp"),
        P(None, "exp"),
        P(),
        P("exp", None, "ctx"),
        P("exp", None, "ctx"),
        P("exp", "ctx", None),
        P("ctx", None),
        P(),
    )
    out_specs = P("exp", "ctx", None)
    return jax.shard_map(body, mesh=mesh, in_specs=in_specs, out_specs=out_specs, check_vma=False)
```

```python
import functools
import math

import jax
import jax.numpy as jnp
from jax import lax
from jax.experimental import pallas as pl
from jax.experimental.pallas import tpu as pltpu
from jax.sharding import PartitionSpec as P

HD = 128
BLK = 128
ROWS_Y = 4
ANY = pl.BlockSpec(memory_space=pl.ANY)
VM = pl.BlockSpec(memory_space=pltpu.VMEM)
MESH = pl.DeviceIdType.MESH
DMA = pltpu.SemaphoreType.DMA


def place(ny):
    me = lax.axis_index("ctx")
    return lax.div(me, 2 * ny), lax.rem(lax.div(me, 2), ny), lax.rem(me, 2)


def greet(peers):
    barrier = pltpu.get_barrier_semaphore()
    for peer in peers:
        pl.semaphore_signal(barrier, inc=1, device_id=peer, device_id_type=MESH)
    pl.semaphore_wait(barrier, len(peers))


def remote(src, dst, send, recv, peer):
    return pltpu.make_async_remote_copy(
        src_ref=src, dst_ref=dst, send_sem=send, recv_sem=recv, device_id=peer, device_id_type=MESH
    )


def spread(nz, ny, at, peer, g_ref, large, small, sems):
    z, y, c = at
    y_send, y_recv, f_send, f_recv, b_send, b_recv, sz_send, sz_recv, sy_send, sy_recv = sems
    up, down = peer(lax.rem(z + 1, nz), y, c), peer(lax.rem(z + nz - 1, nz), y, c)
    half = nz // 2
    pair = ny // 2
    far_z = sorted(range(1, nz), key=lambda d: -min(d, nz - d))
    far_y = sorted(range(1, ny), key=lambda d: -min(d, ny - d))
    pending = []

    def go(ref, send, recv, who):
        copy = remote(ref, ref, send, recv, who)
        copy.start()
        pending.append(copy)

    def arrived(ref, send, recv, who):
        remote(ref, ref, send, recv, who).wait_recv()

    for d in far_y:
        go(g_ref.at[(z, y) + large], y_send.at[d], y_recv.at[d], peer(z, lax.rem(y + d, ny), c))
    for d in far_z:
        go(g_ref.at[(z, y) + small], sz_send.at[d], sz_recv.at[d], peer(lax.rem(z + d, nz), y, c))
    for d in reversed(far_y):
        yy = lax.rem(y + ny - d, ny)
        arrived(g_ref.at[(z, yy) + large], y_send.at[d], y_recv.at[d], peer(z, yy, c))

    def piece(s, k):
        return g_ref.at[(lax.rem(z + nz + s, nz), pl.ds(k * pair, pair)) + large]

    def onward(s, k):
        if s < half - 1 or (s == half - 1 and k == 0):
            go(piece(-s, k), f_send.at[s, k], f_recv.at[s, k], up)

    def backward(s, k):
        if s < half - 1 or (s == half - 1 and k == 1):
            go(piece(s, k), b_send.at[s, k], b_recv.at[s, k], down)

    for k in range(2):
        onward(0, k)
        backward(0, k)
    for d in reversed(far_z):
        zz = lax.rem(z + nz - d, nz)
        arrived(g_ref.at[(zz, y) + small], sz_send.at[d], sz_recv.at[d], peer(zz, y, c))
    for d in far_y:
        ref = g_ref.at[(slice(None), y) + small]
        go(ref, sy_send.at[d], sy_recv.at[d], peer(z, lax.rem(y + d, ny), c))
    for s in range(1, half + 1):
        for k in range(2):
            if s < half or k == 0:
                arrived(piece(-s, k), f_send.at[s - 1, k], f_recv.at[s - 1, k], down)
                onward(s, k)
            if s < half or k == 1:
                arrived(piece(s, k), b_send.at[s - 1, k], b_recv.at[s - 1, k], up)
                backward(s, k)
    for d in reversed(far_y):
        yy = lax.rem(y + ny - d, ny)
        ref = g_ref.at[(slice(None), yy) + small]
        arrived(ref, sy_send.at[d], sy_recv.at[d], peer(z, yy, c))
    return pending


def ctx_peer(ny):
    return lambda z, y, c: {"ctx": (z * ny + y) * 2 + c}


def ring_peers(nz, ny, at, peer):
    z, y, c = at
    out = [peer(z, lax.rem(y + d, ny), c) for d in range(1, ny)]
    return out + [peer(lax.rem(z + d, nz), y, c) for d in range(1, nz)]


def keys_kernel(
    nz, ny, q_ref, kv_ref, w0, w1, w2, qo_ref, g_ref, p0, p1, p2, own, d_send, d_recv, *sems
):
    at = z, y, c = place(ny)
    peer = ctx_peer(ny)
    other = peer(z, y, 1 - c)
    greet(ring_peers(nz, ny, at, peer) + [other])
    swap_kv = remote(kv_ref.at[1 - c], g_ref.at[z, y, c], d_send.at[0], d_recv.at[0], other)
    swap_q = remote(q_ref.at[1 - c], qo_ref.at[c], d_send.at[1], d_recv.at[1], other)
    swap_kv.start()
    swap_q.start()
    keep_kv = pltpu.make_async_copy(kv_ref.at[c], g_ref.at[z, y, c], own.at[0])
    keep_q = pltpu.make_async_copy(q_ref.at[c], qo_ref.at[c], own.at[1])
    keep_kv.start()
    keep_q.start()
    keep_kv.wait()
    got = g_ref.at[z, y, 1 - c]
    remote(got, got, d_send.at[0], d_recv.at[0], other).wait_recv()
    weights = [
        remote(src, dst, d_send.at[2 + i], d_recv.at[2 + i], other)
        for i, (src, dst) in enumerate([(w0, p0), (w1, p1), (w2, p2)])
    ]
    for copy in weights:
        copy.start()
    cut = g_ref.shape[3] * 3 // 4
    large = (slice(None), pl.ds(0, cut))
    small = (slice(None), pl.ds(cut, g_ref.shape[3] - cut))
    pending = spread(nz, ny, at, peer, g_ref, large, small, sems)
    for copy in pending:
        copy.wait_send()
    for copy in weights:
        copy.wait()
    keep_q.wait()
    got_q = qo_ref.at[1 - c]
    remote(got_q, got_q, d_send.at[1], d_recv.at[1], other).wait_recv()
    swap_kv.wait_send()
    swap_q.wait_send()


def rows_kernel(nz, ny, x_ref, g_ref, own, *sems):
    at = z, y, c = place(ny)
    peer = ctx_peer(ny)
    keep = pltpu.make_async_copy(x_ref, g_ref.at[z, y], own)
    keep.start()
    greet(ring_peers(nz, ny, at, peer))
    keep.wait()
    cut = g_ref.shape[3] * 3 // 4
    large = (slice(None), pl.ds(0, cut))
    small = (slice(None), pl.ds(cut, g_ref.shape[3] - cut))
    for copy in spread(nz, ny, at, peer, g_ref, large, small, sems):
        copy.wait_send()


def ring_sems(nz, ny):
    return [DMA((ny,))] * 2 + [DMA((nz // 2, 2))] * 4 + [DMA((nz,))] * 2 + [DMA((ny,))] * 2


def gather_keys(q2, kv2, weights, nz, ny):
    return pl.pallas_call(
        functools.partial(keys_kernel, nz, ny),
        out_shape=(
            jax.ShapeDtypeStruct(q2.shape, q2.dtype),
            jax.ShapeDtypeStruct((nz, ny) + kv2.shape, kv2.dtype),
            *(jax.ShapeDtypeStruct(w.shape, w.dtype) for w in weights),
        ),
        in_specs=[VM, VM, ANY, ANY, ANY],
        out_specs=(VM, VM, ANY, ANY, ANY),
        scratch_shapes=[DMA((2,)), DMA((5,)), DMA((5,))] + ring_sems(nz, ny),
        compiler_params=pltpu.CompilerParams(collective_id=0, has_side_effects=True),
    )(q2, kv2, *weights)


def gather_rows(x, nz, ny):
    return pl.pallas_call(
        functools.partial(rows_kernel, nz, ny),
        out_shape=jax.ShapeDtypeStruct((nz, ny) + x.shape, x.dtype),
        in_specs=[VM],
        out_specs=VM,
        scratch_shapes=[DMA] + ring_sems(nz, ny),
        compiler_params=pltpu.CompilerParams(collective_id=1, has_side_effects=True),
    )(x)


def heads_kernel(ny, ne, a_ref, o_ref, own, send, recv):
    z, y, c = place(ny)
    e = lax.axis_index("exp")

    def peer(de, dc):
        return {
            "ctx": (z * ny + y) * 2 + lax.rem(c + dc, 2),
            "exp": lax.rem(e + de, ne),
        }

    others = [(de, dc) for de in range(ne) for dc in range(2) if de or dc]
    keep = pltpu.make_async_copy(a_ref.at[c], o_ref.at[e, c], own)
    keep.start()
    greet([peer(de, dc) for de, dc in others])
    copies = []
    for de, dc in others:
        copy = remote(
            a_ref.at[lax.rem(c + dc, 2)], o_ref.at[e, c], send.at[de, dc], recv.at[de, dc], peer(de, dc)
        )
        copy.start()
        copies.append(copy)
    keep.wait()
    for de, dc in others:
        got = o_ref.at[lax.rem(e + ne - de, ne), lax.rem(c + dc, 2)]
        remote(got, got, send.at[de, dc], recv.at[de, dc], peer(de, dc)).wait_recv()
    for copy in copies:
        copy.wait_send()


def share_heads(a, ny, ne):
    return pl.pallas_call(
        functools.partial(heads_kernel, ny, ne),
        out_shape=jax.ShapeDtypeStruct((ne,) + a.shape, a.dtype),
        in_specs=[VM],
        out_specs=VM,
        scratch_shapes=[DMA, DMA((ne, 2)), DMA((ne, 2))],
        compiler_params=pltpu.CompilerParams(collective_id=2, has_side_effects=True),
    )(a)


def pieces_kernel(ne, x_ref, o_ref, own, send, recv):
    e = lax.axis_index("exp")
    keep = pltpu.make_async_copy(x_ref.at[e], o_ref.at[e], own)
    keep.start()
    greet([{"exp": lax.rem(e + de, ne)} for de in range(1, ne)])
    copies = []
    for de in range(1, ne):
        to = lax.rem(e + de, ne)
        copy = remote(x_ref.at[to], o_ref.at[e], send.at[de], recv.at[de], {"exp": to})
        copy.start()
        copies.append(copy)
    keep.wait()
    for de in range(1, ne):
        back = lax.rem(e + ne - de, ne)
        got = o_ref.at[back]
        remote(got, got, send.at[de], recv.at[de], {"exp": back}).wait_recv()
    for copy in copies:
        copy.wait_send()


def share_pieces(x, ne):
    return pl.pallas_call(
        functools.partial(pieces_kernel, ne),
        out_shape=jax.ShapeDtypeStruct(x.shape, x.dtype),
        in_specs=[VM],
        out_specs=VM,
        scratch_shapes=[DMA, DMA((ne,)), DMA((ne,))],
        compiler_params=pltpu.CompilerParams(collective_id=4, has_side_effects=True),
    )(x)


def sum_kernel(nz, ny, t_ref, h_ref, o_ref, rz, ry, uz, uy, vz, vy, *sems):
    z, y, c = place(ny)
    rz_send, rz_recv, ry_send, ry_recv, vz_send, vz_recv, vy_send, vy_recv = sems
    half = t_ref.shape[-1] // 2
    left, right = pl.ds(0, half), pl.ds(half, half)
    peer = ctx_peer(ny)
    far_z = sorted(range(1, nz), key=lambda d: -min(d, nz - d))
    far_y = sorted(range(1, ny), key=lambda d: -min(d, ny - d))
    to_z = {d: lax.rem(z + d, nz) for d in far_z}
    to_y = {d: lax.rem(y + d, ny) for d in far_y}
    greet([peer(to_z[d], y, c) for d in far_z] + [peer(z, to_y[d], c) for d in far_y])

    def send(src, dst, sends, recvs, who):
        copy = remote(src, dst, sends, recvs, who)
        copy.start()
        return copy

    by_z = [
        send(t_ref.at[to_z[d], :, :, left], rz.at[d], rz_send.at[d], rz_recv.at[d], peer(to_z[d], y, c))
        for d in far_z
    ]
    by_y = [
        send(t_ref.at[:, to_y[d], :, right], ry.at[d], ry_send.at[d], ry_recv.at[d], peer(z, to_y[d], c))
        for d in far_y
    ]
    total = t_ref[z, :, :, :half].astype(jnp.float32)
    for d, copy in zip(far_z, by_z):
        copy.wait_recv()
        total = total + rz[d].astype(jnp.float32)
    uz[...] = total.astype(jnp.bfloat16)
    then_y = [
        send(uz.at[to_y[d]], vz.at[d], vz_send.at[d], vz_recv.at[d], peer(z, to_y[d], c)) for d in far_y
    ]
    total = t_ref[:, y, :, half:].astype(jnp.float32)
    for d, copy in zip(far_y, by_y):
        copy.wait_recv()
        total = total + ry[d].astype(jnp.float32)
    uy[...] = total.astype(jnp.bfloat16)
    then_z = [
        send(uy.at[to_z[d]], vy.at[d], vy_send.at[d], vy_recv.at[d], peer(to_z[d], y, c)) for d in far_z
    ]
    result = h_ref[:, :half].astype(jnp.float32) + uz[y].astype(jnp.float32)
    for d, copy in zip(far_y, then_y):
        copy.wait_recv()
        result = result + vz[d].astype(jnp.float32)
    o_ref[:, :half] = result.astype(jnp.bfloat16)
    result = h_ref[:, half:].astype(jnp.float32) + uy[z].astype(jnp.float32)
    for d, copy in zip(far_z, then_z):
        copy.wait_recv()
        result = result + vy[d].astype(jnp.float32)
    o_ref[:, half:] = result.astype(jnp.bfloat16)
    for copy in by_z + by_y + then_y + then_z:
        copy.wait_send()


def sum_rows(terms, own, nz, ny):
    rows, width = own.shape
    half = width // 2
    t = terms.reshape(nz, ny, rows, width)

    def buf(*lead):
        return pltpu.VMEM(lead + (rows, half), jnp.bfloat16)

    return pl.pallas_call(
        functools.partial(sum_kernel, nz, ny),
        out_shape=jax.ShapeDtypeStruct(own.shape, own.dtype),
        in_specs=[VM, VM],
        out_specs=VM,
        scratch_shapes=[buf(nz, ny), buf(ny, nz), buf(ny), buf(nz), buf(ny), buf(nz)]
        + [DMA((n,)) for n in (nz, nz, ny, ny, ny, ny, nz, nz)],
        compiler_params=pltpu.CompilerParams(collective_id=3, has_side_effects=True),
    )(t, own)


def body(
    residual, queries, keys, values, out_proj, norm_gain, w_gate, w_up, w_down, routes, block_mask
):
    local_tokens = residual.shape[0]
    blocks_all = block_mask.shape[0]
    expert_count = lax.axis_size("exp")
    ny = ROWS_Y
    nz = lax.axis_size("ctx") // (2 * ny)
    per_expert = local_tokens // expert_count
    scaling = 1.0 / math.sqrt(HD)
    ctx_place = lax.axis_index("ctx")
    q2 = queries.reshape(local_tokens, 2, HD).transpose(1, 0, 2)
    kv2 = jnp.concatenate(
        [
            keys.reshape(local_tokens, 2, HD).transpose(1, 0, 2),
            values.reshape(local_tokens, 2, HD).transpose(1, 0, 2),
        ],
        axis=2,
    )
    mine = (w_gate[0], w_up[0], w_down[0])
    q_chip, kv_all, *partner = gather_keys(q2, kv2, mine, nz, ny)
    chip_tokens = 2 * local_tokens
    q_chip = q_chip.reshape(chip_tokens, HD)
    kv_all = kv_all.reshape(-1, 2 * HD)
    count = kv_all.shape[0]
    query_pos = (ctx_place // 2) * chip_tokens + jnp.arange(chip_tokens, dtype=jnp.int32)
    query_blocks = jax.nn.one_hot(query_pos // BLK, blocks_all, dtype=jnp.float32)
    query_mask = jnp.dot(query_blocks, block_mask.astype(jnp.float32))
    key_pos = jnp.arange(count, dtype=jnp.int32)
    key_blocks = jax.nn.one_hot(key_pos // BLK, blocks_all, dtype=jnp.float32)
    allowed = jnp.dot(query_mask, key_blocks.T) > 0.5
    scores = (
        jnp.einsum("qd,kd->qk", q_chip, kv_all[:, :HD], preferred_element_type=jnp.float32) * scaling
    )
    scores = jnp.where(allowed, scores, -1e30)
    top = jnp.max(scores, axis=1, keepdims=True)
    exponent = jnp.where(allowed, jnp.exp(scores - top), 0.0)
    total = jnp.sum(exponent, axis=1, keepdims=True)
    product = jnp.dot(
        exponent.astype(jnp.bfloat16), kv_all[:, HD:], preferred_element_type=jnp.float32
    )
    attended = (product / total).astype(jnp.bfloat16).reshape(2, local_tokens, HD)
    heads = share_heads(attended, ny, expert_count)
    heads = heads.reshape(2 * expert_count, local_tokens, HD)
    heads = heads.transpose(1, 0, 2).reshape(local_tokens, 2 * expert_count * HD)
    projected = jnp.dot(heads, out_proj, preferred_element_type=jnp.float32)
    hidden = (residual.astype(jnp.float32) + projected).astype(jnp.bfloat16)
    target = routes[:, 0]
    token_ids = jnp.arange(local_tokens, dtype=jnp.int32)
    earlier = (target[:, None] == target[None, :]) & (token_ids[None, :] < token_ids[:, None])
    ranking = jnp.sum(earlier.astype(jnp.int32), axis=1)
    slot_of = target * per_expert + ranking
    slot_ids = jnp.arange(expert_count * per_expert, dtype=jnp.int32)
    placing = (slot_of[None, :] == slot_ids[:, None]).astype(jnp.bfloat16)
    send_buffer = jnp.dot(placing, hidden, preferred_element_type=jnp.float32).astype(jnp.bfloat16)
    send_buffer = send_buffer.reshape(expert_count, per_expert, hidden.shape[1])
    own_rows = share_pieces(send_buffer, expert_count).transpose(1, 0, 2).reshape(per_expert, -1)
    values_f = own_rows.astype(jnp.float32)
    meansq = jnp.mean(values_f * values_f, axis=1, keepdims=True)
    normed_own = (values_f * lax.rsqrt(meansq + 1e-05) * norm_gain).astype(jnp.bfloat16)
    normed_rows = gather_rows(normed_own, nz, ny).reshape(-1, normed_own.shape[1])
    terms = 0.0
    for gate, up, down in (mine, partner):
        gate_v = jnp.dot(normed_rows, gate, preferred_element_type=jnp.float32)
        up_v = jnp.dot(normed_rows, up, preferred_element_type=jnp.float32)
        activ = (jax.nn.silu(gate_v) * up_v).astype(jnp.bfloat16)
        terms = terms + jnp.dot(activ, down, preferred_element_type=jnp.float32)
    terms = terms.astype(jnp.bfloat16)
    return sum_rows(terms, own_rows, nz, ny)[None]


def solution(mesh):
    in_specs = (
        P("ctx", "exp"),
        P("ctx", "exp"),
        P("ctx", "exp"),
        P("ctx", "exp"),
        P(None, "exp"),
        P(),
        P("exp", None, "ctx"),
        P("exp", None, "ctx"),
        P("exp", "ctx", None),
        P("ctx", None),
        P(),
    )
    out_specs = P("exp", "ctx", None)
    return jax.shard_map(body, mesh=mesh, in_specs=in_specs, out_specs=out_specs, check_vma=False)
```

```python
import functools
import math

import jax
import jax.numpy as jnp
from jax import lax
from jax.experimental import pallas as pl
from jax.experimental.pallas import tpu as pltpu
from jax.sharding import PartitionSpec as P

HD = 128
BLK = 128
ROWS_Y = 4
ANY = pl.BlockSpec(memory_space=pl.ANY)
VM = pl.BlockSpec(memory_space=pltpu.VMEM)
MESH = pl.DeviceIdType.MESH
DMA = pltpu.SemaphoreType.DMA


def place(ny):
    me = lax.axis_index("ctx")
    return lax.div(me, 2 * ny), lax.rem(lax.div(me, 2), ny), lax.rem(me, 2)


def greet(peers):
    barrier = pltpu.get_barrier_semaphore()
    for peer in peers:
        pl.semaphore_signal(barrier, inc=1, device_id=peer, device_id_type=MESH)
    pl.semaphore_wait(barrier, len(peers))


def remote(src, dst, send, recv, peer):
    return pltpu.make_async_remote_copy(
        src_ref=src, dst_ref=dst, send_sem=send, recv_sem=recv, device_id=peer, device_id_type=MESH
    )


def spread(nz, ny, at, peer, g_ref, large, small, sems):
    z, y, c = at
    y_send, y_recv, f_send, f_recv, b_send, b_recv, sz_send, sz_recv, sy_send, sy_recv = sems
    up, down = peer(lax.rem(z + 1, nz), y, c), peer(lax.rem(z + nz - 1, nz), y, c)
    half = nz // 2
    pair = ny // 2
    far_z = sorted(range(1, nz), key=lambda d: -min(d, nz - d))
    far_y = sorted(range(1, ny), key=lambda d: -min(d, ny - d))
    pending = []

    def go(ref, send, recv, who):
        copy = remote(ref, ref, send, recv, who)
        copy.start()
        pending.append(copy)

    def arrived(ref, send, recv, who):
        remote(ref, ref, send, recv, who).wait_recv()

    for d in far_y:
        go(g_ref.at[(z, y) + large], y_send.at[d], y_recv.at[d], peer(z, lax.rem(y + d, ny), c))
    for d in far_z:
        go(g_ref.at[(z, y) + small], sz_send.at[d], sz_recv.at[d], peer(lax.rem(z + d, nz), y, c))
    for d in reversed(far_y):
        yy = lax.rem(y + ny - d, ny)
        arrived(g_ref.at[(z, yy) + large], y_send.at[d], y_recv.at[d], peer(z, yy, c))

    def piece(s, k):
        return g_ref.at[(lax.rem(z + nz + s, nz), pl.ds(k * pair, pair)) + large]

    def onward(s, k):
        if s < half - 1 or (s == half - 1 and k == 0):
            go(piece(-s, k), f_send.at[s, k], f_recv.at[s, k], up)

    def backward(s, k):
        if s < half - 1 or (s == half - 1 and k == 1):
            go(piece(s, k), b_send.at[s, k], b_recv.at[s, k], down)

    for k in range(2):
        onward(0, k)
        backward(0, k)
    for d in reversed(far_z):
        zz = lax.rem(z + nz - d, nz)
        arrived(g_ref.at[(zz, y) + small], sz_send.at[d], sz_recv.at[d], peer(zz, y, c))
    for d in far_y:
        ref = g_ref.at[(slice(None), y) + small]
        go(ref, sy_send.at[d], sy_recv.at[d], peer(z, lax.rem(y + d, ny), c))
    for s in range(1, half + 1):
        for k in range(2):
            if s < half or k == 0:
                arrived(piece(-s, k), f_send.at[s - 1, k], f_recv.at[s - 1, k], down)
                onward(s, k)
            if s < half or k == 1:
                arrived(piece(s, k), b_send.at[s - 1, k], b_recv.at[s - 1, k], up)
                backward(s, k)
    for d in reversed(far_y):
        yy = lax.rem(y + ny - d, ny)
        ref = g_ref.at[(slice(None), yy) + small]
        arrived(ref, sy_send.at[d], sy_recv.at[d], peer(z, yy, c))
    return pending


def ctx_peer(ny):
    return lambda z, y, c: {"ctx": (z * ny + y) * 2 + c}


def ring_peers(nz, ny, at, peer):
    z, y, c = at
    out = [peer(z, lax.rem(y + d, ny), c) for d in range(1, ny)]
    return out + [peer(lax.rem(z + d, nz), y, c) for d in range(1, nz)]


def keys_kernel(
    nz, ny, q_ref, kv_ref, w0, w1, w2, qo_ref, g_ref, p0, p1, p2, own, d_send, d_recv, *sems
):
    at = z, y, c = place(ny)
    peer = ctx_peer(ny)
    other = peer(z, y, 1 - c)
    greet(ring_peers(nz, ny, at, peer) + [other])
    swap_kv = remote(kv_ref.at[1 - c], g_ref.at[z, y, c], d_send.at[0], d_recv.at[0], other)
    swap_q = remote(q_ref.at[1 - c], qo_ref.at[c], d_send.at[1], d_recv.at[1], other)
    swap_kv.start()
    swap_q.start()
    keep_kv = pltpu.make_async_copy(kv_ref.at[c], g_ref.at[z, y, c], own.at[0])
    keep_q = pltpu.make_async_copy(q_ref.at[c], qo_ref.at[c], own.at[1])
    keep_kv.start()
    keep_q.start()
    keep_kv.wait()
    got = g_ref.at[z, y, 1 - c]
    remote(got, got, d_send.at[0], d_recv.at[0], other).wait_recv()
    weights = [
        remote(src, dst, d_send.at[2 + i], d_recv.at[2 + i], other)
        for i, (src, dst) in enumerate([(w0, p0), (w1, p1), (w2, p2)])
    ]
    for copy in weights:
        copy.start()
    cut = g_ref.shape[3] * 3 // 4
    large = (slice(None), pl.ds(0, cut))
    small = (slice(None), pl.ds(cut, g_ref.shape[3] - cut))
    pending = spread(nz, ny, at, peer, g_ref, large, small, sems)
    for copy in pending:
        copy.wait_send()
    for copy in weights:
        copy.wait()
    keep_q.wait()
    got_q = qo_ref.at[1 - c]
    remote(got_q, got_q, d_send.at[1], d_recv.at[1], other).wait_recv()
    swap_kv.wait_send()
    swap_q.wait_send()


def ring_sems(nz, ny):
    return [DMA((ny,))] * 2 + [DMA((nz // 2, 2))] * 4 + [DMA((nz,))] * 2 + [DMA((ny,))] * 2


def gather_keys(q2, kv2, weights, nz, ny):
    return pl.pallas_call(
        functools.partial(keys_kernel, nz, ny),
        out_shape=(
            jax.ShapeDtypeStruct(q2.shape, q2.dtype),
            jax.ShapeDtypeStruct((nz, ny) + kv2.shape, kv2.dtype),
            *(jax.ShapeDtypeStruct(w.shape, w.dtype) for w in weights),
        ),
        in_specs=[VM, VM, ANY, ANY, ANY],
        out_specs=(VM, VM, ANY, ANY, ANY),
        scratch_shapes=[DMA((2,)), DMA((5,)), DMA((5,))] + ring_sems(nz, ny),
        compiler_params=pltpu.CompilerParams(collective_id=0, has_side_effects=True),
    )(q2, kv2, *weights)


def swap_heads(ny, ne, a_ref, o_ref, own, send, recv):
    z, y, c = place(ny)
    e = lax.axis_index("exp")
    keep = pltpu.make_async_copy(a_ref.at[c], o_ref.at[e, c], own)
    keep.start()
    others = [(de, dc) for de in range(ne) for dc in range(2) if de or dc]
    copies = []
    for de, dc in others:
        to = {"ctx": (z * ny + y) * 2 + lax.rem(c + dc, 2), "exp": lax.rem(e + de, ne)}
        copy = remote(a_ref.at[lax.rem(c + dc, 2)], o_ref.at[e, c], send.at[de, dc], recv.at[de, dc], to)
        copy.start()
        copies.append(copy)
    keep.wait()
    for de, dc in others:
        back = lax.rem(e + ne - de, ne)
        got = o_ref.at[back, lax.rem(c + dc, 2)]
        remote(got, got, send.at[de, dc], recv.at[de, dc], {"exp": back}).wait_recv()
    return copies


def swap_pieces(ne, x_ref, o_ref, own, send, recv):
    e = lax.axis_index("exp")
    keep = pltpu.make_async_copy(x_ref.at[e], o_ref.at[e], own)
    keep.start()
    copies = []
    for de in range(1, ne):
        to = lax.rem(e + de, ne)
        copy = remote(x_ref.at[to], o_ref.at[e], send.at[de], recv.at[de], {"exp": to})
        copy.start()
        copies.append(copy)
    keep.wait()
    for de in range(1, ne):
        back = lax.rem(e + ne - de, ne)
        got = o_ref.at[back]
        remote(got, got, send.at[de], recv.at[de], {"exp": back}).wait_recv()
    return copies


def sum_rows(nz, ny, t_ref, own_rows, o_ref, rz, ry, uz, uy, vz, vy, sems):
    z, y, c = place(ny)
    rz_send, rz_recv, ry_send, ry_recv, vz_send, vz_recv, vy_send, vy_recv = sems
    half = t_ref.shape[-1] // 2
    left, right = pl.ds(0, half), pl.ds(half, half)
    peer = ctx_peer(ny)
    far_z = sorted(range(1, nz), key=lambda d: -min(d, nz - d))
    far_y = sorted(range(1, ny), key=lambda d: -min(d, ny - d))
    to_z = {d: lax.rem(z + d, nz) for d in far_z}
    to_y = {d: lax.rem(y + d, ny) for d in far_y}

    def send(src, dst, sends, recvs, who):
        copy = remote(src, dst, sends, recvs, who)
        copy.start()
        return copy

    by_z = [
        send(t_ref.at[to_z[d], :, :, left], rz.at[d], rz_send.at[d], rz_recv.at[d], peer(to_z[d], y, c))
        for d in far_z
    ]
    by_y = [
        send(t_ref.at[:, to_y[d], :, right], ry.at[d], ry_send.at[d], ry_recv.at[d], peer(z, to_y[d], c))
        for d in far_y
    ]
    total = t_ref[z, :, :, :half].astype(jnp.float32)
    for d, copy in zip(far_z, by_z):
        copy.wait_recv()
        total = total + rz[d].astype(jnp.float32)
    uz[...] = total.astype(jnp.bfloat16)
    then_y = [
        send(uz.at[to_y[d]], vz.at[d], vz_send.at[d], vz_recv.at[d], peer(z, to_y[d], c)) for d in far_y
    ]
    total = t_ref[:, y, :, half:].astype(jnp.float32)
    for d, copy in zip(far_y, by_y):
        copy.wait_recv()
        total = total + ry[d].astype(jnp.float32)
    uy[...] = total.astype(jnp.bfloat16)
    then_z = [
        send(uy.at[to_z[d]], vy.at[d], vy_send.at[d], vy_recv.at[d], peer(to_z[d], y, c)) for d in far_z
    ]
    result = own_rows[:, :half] + uz[y].astype(jnp.float32)
    for d, copy in zip(far_y, then_y):
        copy.wait_recv()
        result = result + vz[d].astype(jnp.float32)
    o_ref[:, :half] = result.astype(jnp.bfloat16)
    result = own_rows[:, half:] + uy[z].astype(jnp.float32)
    for d, copy in zip(far_z, then_z):
        copy.wait_recv()
        result = result + vy[d].astype(jnp.float32)
    o_ref[:, half:] = result.astype(jnp.bfloat16)
    return by_z + by_y + then_y + then_z


def layer_kernel(
    nz, ny, ne, a_ref, res_ref, proj_ref, place_ref, gain_ref, w0, w1, w2, p0, p1, p2, o_ref,
    heads, pieces, own, g_buf, rows_buf, t_buf, b0, b1, b2, c0, c1, c2,
    rz, ry, uz, uy, vz, vy, local, h_send, h_recv, p_send, p_recv, *sems
):
    at = z, y, c = place(ny)
    e = lax.axis_index("exp")
    peer = ctx_peer(ny)
    loads = [
        pltpu.make_async_copy(src, dst, local.at[2 + i])
        for i, (src, dst) in enumerate(
            [(w0, b0), (w1, b1), (w2, b2), (p0, c0), (p1, c1), (p2, c2)]
        )
    ]
    for copy in loads:
        copy.start()
    greet(
        ring_peers(nz, ny, at, peer)
        + [
            {"ctx": (z * ny + y) * 2 + lax.rem(c + dc, 2), "exp": lax.rem(e + de, ne)}
            for de in range(ne)
            for dc in range(2)
            if de or dc
        ]
    )
    sent = swap_heads(ny, ne, a_ref, heads, local.at[0], h_send, h_recv)
    hidden = res_ref[...].astype(jnp.float32)
    for i in range(ne):
        for j in range(2):
            h = 2 * i + j
            hidden = hidden + jnp.dot(
                heads[i, j], proj_ref[h * HD : (h + 1) * HD, :], preferred_element_type=jnp.float32
            )
    hidden = hidden.astype(jnp.bfloat16)
    slots = jnp.dot(place_ref[...], hidden, preferred_element_type=jnp.float32)
    pieces[...] = slots.reshape(pieces.shape).astype(jnp.bfloat16)
    sent += swap_pieces(ne, pieces, own, local.at[1], p_send, p_recv)
    part = own.shape[2]
    width = ne * part
    own_f = [own[i].astype(jnp.float32) for i in range(ne)]
    square = own_f[0] * own_f[0]
    for v in own_f[1:]:
        square = square + v * v
    inv = lax.rsqrt(jnp.sum(square, axis=1, keepdims=True) / width + 1e-05)
    for i, v in enumerate(own_f):
        cols = slice(i * part, (i + 1) * part)
        g_buf[z, y, :, cols] = (v * inv * gain_ref[:, cols]).astype(jnp.bfloat16)
    cut = width * 3 // 4
    large = (slice(None), pl.ds(0, cut))
    small = (slice(None), pl.ds(cut, width - cut))
    sent += spread(nz, ny, at, peer, g_buf, large, small, sems[:10])
    count = rows_buf.shape[0]
    rows_buf[...] = g_buf[...].astype(jnp.float32).reshape(count, width).astype(jnp.bfloat16)
    for copy in loads:
        copy.wait()
    rows = rows_buf[...]
    acts = []
    for gate, up in ((b0, b1), (c0, c1)):
        gate_v = jnp.dot(rows, gate[...], preferred_element_type=jnp.float32)
        up_v = jnp.dot(rows, up[...], preferred_element_type=jnp.float32)
        acts.append((gate_v / (1.0 + jnp.exp(-gate_v)) * up_v).astype(jnp.bfloat16))
    step = width // 4
    for i in range(4):
        cols = slice(i * step, (i + 1) * step)
        terms = jnp.dot(acts[0], b2[:, cols], preferred_element_type=jnp.float32)
        terms = terms + jnp.dot(acts[1], c2[:, cols], preferred_element_type=jnp.float32)
        t_buf[:, :, :, cols] = terms.reshape(t_buf.shape[:3] + (step,)).astype(jnp.bfloat16)
    own_rows = jnp.concatenate([own[i].astype(jnp.float32) for i in range(ne)], axis=1)
    sent += sum_rows(nz, ny, t_buf, own_rows, o_ref, rz, ry, uz, uy, vz, vy, sems[10:])
    for copy in sent:
        copy.wait_send()


def rest(attended, residual, out_proj, placing, gain, mine, partner, nz, ny, ne):
    tokens, part = residual.shape
    rows, width = tokens // ne, ne * part
    half = width // 2
    units = mine[0].shape[1]

    def buf(*shape):
        return pltpu.VMEM(shape, jnp.bfloat16)

    weights = [buf(width, units), buf(width, units), buf(units, width)]
    return pl.pallas_call(
        functools.partial(layer_kernel, nz, ny, ne),
        out_shape=jax.ShapeDtypeStruct((rows, width), jnp.bfloat16),
        in_specs=[VM] * 5 + [ANY] * 6,
        out_specs=VM,
        scratch_shapes=[
            buf(ne, 2, tokens, HD),
            buf(ne, rows, part),
            buf(ne, rows, part),
            buf(nz, ny, rows, width),
            buf(nz * ny * rows, width),
            buf(nz, ny, rows, width),
            *weights,
            *weights,
            buf(nz, ny, rows, half),
            buf(ny, nz, rows, half),
            buf(ny, rows, half),
            buf(nz, rows, half),
            buf(ny, rows, half),
            buf(nz, rows, half),
            DMA((8,)),
            DMA((ne, 2)),
            DMA((ne, 2)),
            DMA((ne,)),
            DMA((ne,)),
            *ring_sems(nz, ny),
            *(DMA((n,)) for n in (nz, nz, ny, ny, ny, ny, nz, nz)),
        ],
        compiler_params=pltpu.CompilerParams(collective_id=1, has_side_effects=True),
    )(attended, residual, out_proj, placing, gain, *mine, *partner)


def body(
    residual, queries, keys, values, out_proj, norm_gain, w_gate, w_up, w_down, routes, block_mask
):
    local_tokens = residual.shape[0]
    blocks_all = block_mask.shape[0]
    expert_count = lax.axis_size("exp")
    ny = ROWS_Y
    nz = lax.axis_size("ctx") // (2 * ny)
    per_expert = local_tokens // expert_count
    scaling = 1.0 / math.sqrt(HD)
    ctx_place = lax.axis_index("ctx")
    q2 = queries.reshape(local_tokens, 2, HD).transpose(1, 0, 2)
    kv2 = jnp.concatenate(
        [
            keys.reshape(local_tokens, 2, HD).transpose(1, 0, 2),
            values.reshape(local_tokens, 2, HD).transpose(1, 0, 2),
        ],
        axis=2,
    )
    mine = (w_gate[0], w_up[0], w_down[0])
    q_chip, kv_all, *partner = gather_keys(q2, kv2, mine, nz, ny)
    chip_tokens = 2 * local_tokens
    q_chip = q_chip.reshape(chip_tokens, HD)
    kv_all = kv_all.reshape(-1, 2 * HD)
    count = kv_all.shape[0]
    query_pos = (ctx_place // 2) * chip_tokens + jnp.arange(chip_tokens, dtype=jnp.int32)
    query_blocks = jax.nn.one_hot(query_pos // BLK, blocks_all, dtype=jnp.float32)
    query_mask = jnp.dot(query_blocks, block_mask.astype(jnp.float32))
    key_pos = jnp.arange(count, dtype=jnp.int32)
    key_blocks = jax.nn.one_hot(key_pos // BLK, blocks_all, dtype=jnp.float32)
    allowed = jnp.dot(query_mask, key_blocks.T) > 0.5
    scores = (
        jnp.einsum("qd,kd->qk", q_chip, kv_all[:, :HD], preferred_element_type=jnp.float32) * scaling
    )
    scores = jnp.where(allowed, scores, -1e30)
    top = jnp.max(scores, axis=1, keepdims=True)
    exponent = jnp.where(allowed, jnp.exp(scores - top), 0.0)
    total = jnp.sum(exponent, axis=1, keepdims=True)
    product = jnp.dot(
        exponent.astype(jnp.bfloat16), kv_all[:, HD:], preferred_element_type=jnp.float32
    )
    attended = (product / total).astype(jnp.bfloat16).reshape(2, local_tokens, HD)
    target = routes[:, 0]
    token_ids = jnp.arange(local_tokens, dtype=jnp.int32)
    earlier = (target[:, None] == target[None, :]) & (token_ids[None, :] < token_ids[:, None])
    ranking = jnp.sum(earlier.astype(jnp.int32), axis=1)
    slot_of = target * per_expert + ranking
    slot_ids = jnp.arange(expert_count * per_expert, dtype=jnp.int32)
    placing = (slot_of[None, :] == slot_ids[:, None]).astype(jnp.bfloat16)
    return rest(
        attended, residual, out_proj, placing, norm_gain[None], mine, partner, nz, ny, expert_count
    )[None]


def solution(mesh):
    in_specs = (
        P("ctx", "exp"),
        P("ctx", "exp"),
        P("ctx", "exp"),
        P("ctx", "exp"),
        P(None, "exp"),
        P(),
        P("exp", None, "ctx"),
        P("exp", None, "ctx"),
        P("exp", "ctx", None),
        P("ctx", None),
        P(),
    )
    out_specs = P("exp", "ctx", None)
    return jax.shard_map(body, mesh=mesh, in_specs=in_specs, out_specs=out_specs, check_vma=False)
```

```python
import functools
import math

import jax
import jax.numpy as jnp
from jax import lax
from jax.experimental import pallas as pl
from jax.experimental.pallas import tpu as pltpu
from jax.sharding import PartitionSpec as P

HD = 128
BLK = 128
ROWS_Y = 4
ANY = pl.BlockSpec(memory_space=pl.ANY)
VM = pl.BlockSpec(memory_space=pltpu.VMEM)
MESH = pl.DeviceIdType.MESH
DMA = pltpu.SemaphoreType.DMA


def place(ny):
    me = lax.axis_index("ctx")
    return lax.div(me, 2 * ny), lax.rem(lax.div(me, 2), ny), lax.rem(me, 2)


def greet(peers):
    barrier = pltpu.get_barrier_semaphore()
    for peer in peers:
        pl.semaphore_signal(barrier, inc=1, device_id=peer, device_id_type=MESH)
    pl.semaphore_wait(barrier, len(peers))


def remote(src, dst, send, recv, peer):
    return pltpu.make_async_remote_copy(
        src_ref=src, dst_ref=dst, send_sem=send, recv_sem=recv, device_id=peer, device_id_type=MESH
    )


def spread(nz, ny, at, peer, g_ref, large, small, sems):
    z, y, c = at
    y_send, y_recv, f_send, f_recv, b_send, b_recv, sz_send, sz_recv, sy_send, sy_recv = sems
    up, down = peer(lax.rem(z + 1, nz), y, c), peer(lax.rem(z + nz - 1, nz), y, c)
    half = nz // 2
    pair = ny // 2
    far_z = sorted(range(1, nz), key=lambda d: -min(d, nz - d))
    far_y = sorted(range(1, ny), key=lambda d: -min(d, ny - d))
    pending = []

    def go(ref, send, recv, who):
        copy = remote(ref, ref, send, recv, who)
        copy.start()
        pending.append(copy)

    def arrived(ref, send, recv, who):
        remote(ref, ref, send, recv, who).wait_recv()

    for d in far_y:
        go(g_ref.at[(z, y) + large], y_send.at[d], y_recv.at[d], peer(z, lax.rem(y + d, ny), c))
    for d in far_z:
        go(g_ref.at[(z, y) + small], sz_send.at[d], sz_recv.at[d], peer(lax.rem(z + d, nz), y, c))
    for d in reversed(far_y):
        yy = lax.rem(y + ny - d, ny)
        arrived(g_ref.at[(z, yy) + large], y_send.at[d], y_recv.at[d], peer(z, yy, c))

    def piece(s, k):
        return g_ref.at[(lax.rem(z + nz + s, nz), pl.ds(k * pair, pair)) + large]

    def onward(s, k):
        if s < half - 1 or (s == half - 1 and k == 0):
            go(piece(-s, k), f_send.at[s, k], f_recv.at[s, k], up)

    def backward(s, k):
        if s < half - 1 or (s == half - 1 and k == 1):
            go(piece(s, k), b_send.at[s, k], b_recv.at[s, k], down)

    for k in range(2):
        onward(0, k)
        backward(0, k)
    for d in reversed(far_z):
        zz = lax.rem(z + nz - d, nz)
        arrived(g_ref.at[(zz, y) + small], sz_send.at[d], sz_recv.at[d], peer(zz, y, c))
    for d in far_y:
        ref = g_ref.at[(slice(None), y) + small]
        go(ref, sy_send.at[d], sy_recv.at[d], peer(z, lax.rem(y + d, ny), c))
    for s in range(1, half + 1):
        for k in range(2):
            if s < half or k == 0:
                arrived(piece(-s, k), f_send.at[s - 1, k], f_recv.at[s - 1, k], down)
                onward(s, k)
            if s < half or k == 1:
                arrived(piece(s, k), b_send.at[s - 1, k], b_recv.at[s - 1, k], up)
                backward(s, k)
    for d in reversed(far_y):
        yy = lax.rem(y + ny - d, ny)
        ref = g_ref.at[(slice(None), yy) + small]
        arrived(ref, sy_send.at[d], sy_recv.at[d], peer(z, yy, c))
    return pending


def ctx_peer(ny):
    return lambda z, y, c: {"ctx": (z * ny + y) * 2 + c}


def ring_peers(nz, ny, at, peer):
    z, y, c = at
    out = [peer(z, lax.rem(y + d, ny), c) for d in range(1, ny)]
    return out + [peer(lax.rem(z + d, nz), y, c) for d in range(1, nz)]


def swap_tokens(nz, ny, inputs, q_buf, kv_buf, weights, send, recv, own):
    z, y, c = place(ny)
    other = ctx_peer(ny)(z, y, 1 - c)
    mine = pl.ds(pl.multiple_of(c * HD, HD), HD)
    theirs = pl.ds(pl.multiple_of((1 - c) * HD, HD), HD)
    spots = [
        lambda t: q_buf.at[t],
        lambda t: kv_buf.at[z, y, t, :, pl.ds(0, HD)],
        lambda t: kv_buf.at[z, y, t, :, pl.ds(HD, HD)],
    ]
    sent, kept = [], []
    for i, (x, spot) in enumerate(zip(inputs, spots)):
        copy = remote(x.at[:, theirs], spot(c), send.at[i], recv.at[i], other)
        copy.start()
        sent.append(copy)
        copy = pltpu.make_async_copy(x.at[:, mine], spot(c), own.at[i])
        copy.start()
        kept.append(copy)
    for copy in kept:
        copy.wait()
    for i, spot in enumerate(spots):
        got = spot(1 - c)
        remote(got, got, send.at[i], recv.at[i], other).wait_recv()
    swaps = [
        remote(src, dst, send.at[3 + i], recv.at[3 + i], other) for i, (src, dst) in enumerate(weights)
    ]
    for copy in swaps:
        copy.start()
    return sent, swaps


def attend(nz, q_buf, kv_buf, mask_ref, s_buf, a_buf):
    tokens = q_buf.shape[0] * q_buf.shape[1]
    queries = q_buf[...].reshape(tokens, HD)
    span = s_buf.shape[1] // nz
    top = jnp.full((tokens, 1), -1e30, jnp.float32)
    for i in range(nz):
        cols = slice(i * span, (i + 1) * span)
        keys = kv_buf[i, :, :, :, :HD].reshape(span, HD)
        scores = lax.dot_general(
            queries, keys, (((1,), (1,)), ((), ())), preferred_element_type=jnp.float32
        ) * (1.0 / math.sqrt(HD))
        scores = jnp.where(mask_ref[:, cols] > 0, scores, -1e30)
        s_buf[:, cols] = scores
        top = jnp.maximum(top, jnp.max(scores, axis=1, keepdims=True))
    total = jnp.zeros((tokens, 1), jnp.float32)
    product = jnp.zeros((tokens, HD), jnp.float32)
    for i in range(nz):
        cols = slice(i * span, (i + 1) * span)
        values = kv_buf[i, :, :, :, HD:].reshape(span, HD)
        expo = jnp.where(mask_ref[:, cols] > 0, jnp.exp(s_buf[:, cols] - top), 0.0)
        total = total + jnp.sum(expo, axis=1, keepdims=True)
        product = product + jnp.dot(
            expo.astype(jnp.bfloat16), values, preferred_element_type=jnp.float32
        )
    a_buf[...] = (product / total).astype(jnp.bfloat16).reshape(a_buf.shape)


def ring_sems(nz, ny):
    return [DMA((ny,))] * 2 + [DMA((nz // 2, 2))] * 4 + [DMA((nz,))] * 2 + [DMA((ny,))] * 2


def swap_heads(ny, ne, a_ref, o_ref, own, send, recv):
    z, y, c = place(ny)
    e = lax.axis_index("exp")
    keep = pltpu.make_async_copy(a_ref.at[c], o_ref.at[e, c], own)
    keep.start()
    others = [(de, dc) for de in range(ne) for dc in range(2) if de or dc]
    copies = []
    for de, dc in others:
        to = {"ctx": (z * ny + y) * 2 + lax.rem(c + dc, 2), "exp": lax.rem(e + de, ne)}
        copy = remote(a_ref.at[lax.rem(c + dc, 2)], o_ref.at[e, c], send.at[de, dc], recv.at[de, dc], to)
        copy.start()
        copies.append(copy)
    keep.wait()
    for de, dc in others:
        back = lax.rem(e + ne - de, ne)
        got = o_ref.at[back, lax.rem(c + dc, 2)]
        remote(got, got, send.at[de, dc], recv.at[de, dc], {"exp": back}).wait_recv()
    return copies


def swap_pieces(ne, x_ref, o_ref, own, send, recv):
    e = lax.axis_index("exp")
    keep = pltpu.make_async_copy(x_ref.at[e], o_ref.at[e], own)
    keep.start()
    copies = []
    for de in range(1, ne):
        to = lax.rem(e + de, ne)
        copy = remote(x_ref.at[to], o_ref.at[e], send.at[de], recv.at[de], {"exp": to})
        copy.start()
        copies.append(copy)
    keep.wait()
    for de in range(1, ne):
        back = lax.rem(e + ne - de, ne)
        got = o_ref.at[back]
        remote(got, got, send.at[de], recv.at[de], {"exp": back}).wait_recv()
    return copies


def sum_rows(nz, ny, t_ref, own_rows, o_ref, rz, ry, uz, uy, vz, vy, sems):
    z, y, c = place(ny)
    rz_send, rz_recv, ry_send, ry_recv, vz_send, vz_recv, vy_send, vy_recv = sems
    half = t_ref.shape[-1] // 2
    left, right = pl.ds(0, half), pl.ds(half, half)
    peer = ctx_peer(ny)
    far_z = sorted(range(1, nz), key=lambda d: -min(d, nz - d))
    far_y = sorted(range(1, ny), key=lambda d: -min(d, ny - d))
    to_z = {d: lax.rem(z + d, nz) for d in far_z}
    to_y = {d: lax.rem(y + d, ny) for d in far_y}

    def send(src, dst, sends, recvs, who):
        copy = remote(src, dst, sends, recvs, who)
        copy.start()
        return copy

    by_z = [
        send(t_ref.at[to_z[d], :, :, left], rz.at[d], rz_send.at[d], rz_recv.at[d], peer(to_z[d], y, c))
        for d in far_z
    ]
    by_y = [
        send(t_ref.at[:, to_y[d], :, right], ry.at[d], ry_send.at[d], ry_recv.at[d], peer(z, to_y[d], c))
        for d in far_y
    ]
    total = t_ref[z, :, :, :half].astype(jnp.float32)
    for d, copy in zip(far_z, by_z):
        copy.wait_recv()
        total = total + rz[d].astype(jnp.float32)
    uz[...] = total.astype(jnp.bfloat16)
    then_y = [
        send(uz.at[to_y[d]], vz.at[d], vz_send.at[d], vz_recv.at[d], peer(z, to_y[d], c)) for d in far_y
    ]
    total = t_ref[:, y, :, half:].astype(jnp.float32)
    for d, copy in zip(far_y, by_y):
        copy.wait_recv()
        total = total + ry[d].astype(jnp.float32)
    uy[...] = total.astype(jnp.bfloat16)
    then_z = [
        send(uy.at[to_z[d]], vy.at[d], vy_send.at[d], vy_recv.at[d], peer(to_z[d], y, c)) for d in far_z
    ]
    result = own_rows[:, :half] + uz[y].astype(jnp.float32)
    for d, copy in zip(far_y, then_y):
        copy.wait_recv()
        result = result + vz[d].astype(jnp.float32)
    o_ref[:, :half] = result.astype(jnp.bfloat16)
    result = own_rows[:, half:] + uy[z].astype(jnp.float32)
    for d, copy in zip(far_z, then_z):
        copy.wait_recv()
        result = result + vy[d].astype(jnp.float32)
    o_ref[:, half:] = result.astype(jnp.bfloat16)
    return by_z + by_y + then_y + then_z


def layer_kernel(
    nz, ny, ne, q_ref, k_ref, v_ref, mask_ref, res_ref, proj_ref, place_ref, gain_ref, w0, w1, w2,
    o_ref, q_buf, kv_buf, s_buf, a_buf, heads, pieces, own, g_buf, rows_buf, t_buf, b0, b1, b2, c0, c1, c2,
    rz, ry, uz, uy, vz, vy, local, t_send, t_recv, h_send, h_recv, p_send, p_recv, *sems
):
    at = z, y, c = place(ny)
    e = lax.axis_index("exp")
    peer = ctx_peer(ny)
    loads = [
        pltpu.make_async_copy(src, dst, local.at[2 + i])
        for i, (src, dst) in enumerate(
            [(w0, b0), (w1, b1), (w2, b2)]
        )
    ]
    for copy in loads:
        copy.start()
    greet(
        ring_peers(nz, ny, at, peer)
        + [
            {"ctx": (z * ny + y) * 2 + lax.rem(c + dc, 2), "exp": lax.rem(e + de, ne)}
            for de in range(ne)
            for dc in range(2)
            if de or dc
        ]
    )
    sent, swaps = swap_tokens(
        nz, ny, (q_ref, k_ref, v_ref), q_buf, kv_buf, [(w0, c0), (w1, c1), (w2, c2)],
        t_send, t_recv, local.at[pl.ds(5, 3)],
    )
    cut = kv_buf.shape[3] * 3 // 4
    large = (slice(None), pl.ds(0, cut))
    small = (slice(None), pl.ds(cut, kv_buf.shape[3] - cut))
    sent += spread(nz, ny, at, peer, kv_buf, large, small, sems[:10])
    attend(nz, q_buf, kv_buf, mask_ref, s_buf, a_buf)
    sent += swap_heads(ny, ne, a_buf, heads, local.at[0], h_send, h_recv)
    hidden = res_ref[...].astype(jnp.float32)
    for i in range(ne):
        for j in range(2):
            h = 2 * i + j
            hidden = hidden + jnp.dot(
                heads[i, j], proj_ref[h * HD : (h + 1) * HD, :], preferred_element_type=jnp.float32
            )
    hidden = hidden.astype(jnp.bfloat16)
    slots = jnp.dot(place_ref[...], hidden, preferred_element_type=jnp.float32)
    pieces[...] = slots.reshape(pieces.shape).astype(jnp.bfloat16)
    sent += swap_pieces(ne, pieces, own, local.at[1], p_send, p_recv)
    part = own.shape[2]
    width = ne * part
    own_f = [own[i].astype(jnp.float32) for i in range(ne)]
    square = own_f[0] * own_f[0]
    for v in own_f[1:]:
        square = square + v * v
    inv = lax.rsqrt(jnp.sum(square, axis=1, keepdims=True) / width + 1e-05)
    for i, v in enumerate(own_f):
        cols = slice(i * part, (i + 1) * part)
        g_buf[z, y, :, cols] = (v * inv * gain_ref[:, cols]).astype(jnp.bfloat16)
    cut = width * 3 // 4
    large = (slice(None), pl.ds(0, cut))
    small = (slice(None), pl.ds(cut, width - cut))
    sent += spread(nz, ny, at, peer, g_buf, large, small, sems[10:20])
    count = rows_buf.shape[0]
    rows_buf[...] = g_buf[...].astype(jnp.float32).reshape(count, width).astype(jnp.bfloat16)
    for copy in loads + swaps:
        copy.wait()
    rows = rows_buf[...]
    acts = []
    for gate, up in ((b0, b1), (c0, c1)):
        gate_v = jnp.dot(rows, gate[...], preferred_element_type=jnp.float32)
        up_v = jnp.dot(rows, up[...], preferred_element_type=jnp.float32)
        acts.append((gate_v / (1.0 + jnp.exp(-gate_v)) * up_v).astype(jnp.bfloat16))
    step = width // 4
    for i in range(4):
        cols = slice(i * step, (i + 1) * step)
        terms = jnp.dot(acts[0], b2[:, cols], preferred_element_type=jnp.float32)
        terms = terms + jnp.dot(acts[1], c2[:, cols], preferred_element_type=jnp.float32)
        t_buf[:, :, :, cols] = terms.reshape(t_buf.shape[:3] + (step,)).astype(jnp.bfloat16)
    own_rows = jnp.concatenate([own[i].astype(jnp.float32) for i in range(ne)], axis=1)
    sent += sum_rows(nz, ny, t_buf, own_rows, o_ref, rz, ry, uz, uy, vz, vy, sems[20:])
    for copy in sent:
        copy.wait_send()


def layer(
    queries, keys, values, mask, residual, out_proj, placing, gain, mine, nz, ny, ne
):
    tokens, part = residual.shape
    rows, width = tokens // ne, ne * part
    half = width // 2
    units = mine[0].shape[1]

    def buf(*shape):
        return pltpu.VMEM(shape, jnp.bfloat16)

    weights = [buf(width, units), buf(width, units), buf(units, width)]
    return pl.pallas_call(
        functools.partial(layer_kernel, nz, ny, ne),
        out_shape=jax.ShapeDtypeStruct((rows, width), jnp.bfloat16),
        in_specs=[VM] * 8 + [ANY] * 3,
        out_specs=VM,
        scratch_shapes=[
            buf(2, tokens, HD),
            buf(nz, ny, 2, tokens, 2 * HD),
            pltpu.VMEM((2 * tokens, mask.shape[1]), jnp.float32),
            buf(2, tokens, HD),
            buf(ne, 2, tokens, HD),
            buf(ne, rows, part),
            buf(ne, rows, part),
            buf(nz, ny, rows, width),
            buf(nz * ny * rows, width),
            buf(nz, ny, rows, width),
            *weights,
            *weights,
            buf(nz, ny, rows, half),
            buf(ny, nz, rows, half),
            buf(ny, rows, half),
            buf(nz, rows, half),
            buf(ny, rows, half),
            buf(nz, rows, half),
            DMA((8,)),
            DMA((6,)),
            DMA((6,)),
            DMA((ne, 2)),
            DMA((ne, 2)),
            DMA((ne,)),
            DMA((ne,)),
            *ring_sems(nz, ny),
            *ring_sems(nz, ny),
            *(DMA((n,)) for n in (nz, nz, ny, ny, ny, ny, nz, nz)),
        ],
        compiler_params=pltpu.CompilerParams(collective_id=0, has_side_effects=True),
    )(queries, keys, values, mask, residual, out_proj, placing, gain, *mine)


def body(
    residual, queries, keys, values, out_proj, norm_gain, w_gate, w_up, w_down, routes, block_mask
):
    local_tokens = residual.shape[0]
    expert_count = lax.axis_size("exp")
    ny = ROWS_Y
    nz = lax.axis_size("ctx") // (2 * ny)
    per_expert = local_tokens // expert_count
    chip = lax.axis_index("ctx") // 2
    assert 2 * local_tokens == BLK
    mask = jnp.repeat(lax.dynamic_slice_in_dim(block_mask, chip, 1, 0), BLK, axis=1)
    target = routes[:, 0]
    token_ids = jnp.arange(local_tokens, dtype=jnp.int32)
    earlier = (target[:, None] == target[None, :]) & (token_ids[None, :] < token_ids[:, None])
    ranking = jnp.sum(earlier.astype(jnp.int32), axis=1)
    slot_of = target * per_expert + ranking
    slot_ids = jnp.arange(expert_count * per_expert, dtype=jnp.int32)
    placing = (slot_of[None, :] == slot_ids[:, None]).astype(jnp.bfloat16)
    mine = (w_gate[0], w_up[0], w_down[0])
    return layer(
        queries, keys, values, mask, residual, out_proj, placing, norm_gain[None], mine, nz, ny,
        expert_count,
    )[None]


def solution(mesh):
    in_specs = (
        P("ctx", "exp"),
        P("ctx", "exp"),
        P("ctx", "exp"),
        P("ctx", "exp"),
        P(None, "exp"),
        P(),
        P("exp", None, "ctx"),
        P("exp", None, "ctx"),
        P("exp", "ctx", None),
        P("ctx", None),
        P(),
    )
    out_specs = P("exp", "ctx", None)
    return jax.shard_map(body, mesh=mesh, in_specs=in_specs, out_specs=out_specs, check_vma=False)
```

```python
import functools
import math

import jax
import jax.numpy as jnp
from jax import lax
from jax.experimental import pallas as pl
from jax.experimental.pallas import tpu as pltpu
from jax.sharding import PartitionSpec as P

HD = 128
BLK = 128
ROWS_Y = 4
ANY = pl.BlockSpec(memory_space=pl.ANY)
VM = pl.BlockSpec(memory_space=pltpu.VMEM)
MESH = pl.DeviceIdType.MESH
DMA = pltpu.SemaphoreType.DMA


def place(ny):
    me = lax.axis_index("ctx")
    return lax.div(me, 2 * ny), lax.rem(lax.div(me, 2), ny), lax.rem(me, 2)


def greet(peers):
    barrier = pltpu.get_barrier_semaphore()
    for peer in peers:
        pl.semaphore_signal(barrier, inc=1, device_id=peer, device_id_type=MESH)
    pl.semaphore_wait(barrier, len(peers))


def remote(src, dst, send, recv, peer):
    return pltpu.make_async_remote_copy(
        src_ref=src, dst_ref=dst, send_sem=send, recv_sem=recv, device_id=peer, device_id_type=MESH
    )


def spread(nz, ny, at, peer, g_ref, large, small, sems):
    z, y, c = at
    y_send, y_recv, f_send, f_recv, b_send, b_recv, sz_send, sz_recv, sy_send, sy_recv = sems
    up, down = peer(lax.rem(z + 1, nz), y, c), peer(lax.rem(z + nz - 1, nz), y, c)
    half = nz // 2
    far_z = sorted(range(1, nz), key=lambda d: -min(d, nz - d))
    far_y = sorted(range(1, ny), key=lambda d: -min(d, ny - d))
    pending = []

    def go(ref, send, recv, who):
        copy = remote(ref, ref, send, recv, who)
        copy.start()
        pending.append(copy)

    def arrived(ref, send, recv, who):
        remote(ref, ref, send, recv, who).wait_recv()

    for d in far_y:
        go(g_ref.at[(z, y) + large], y_send.at[d], y_recv.at[d], peer(z, lax.rem(y + d, ny), c))
    for d in far_z:
        go(g_ref.at[(z, y) + small], sz_send.at[d], sz_recv.at[d], peer(lax.rem(z + d, nz), y, c))
    near_y = [0] + far_y[::-1]
    ahead = near_y[: ny // 2]

    def piece(s, k):
        return g_ref.at[(lax.rem(z + nz + s, nz), lax.rem(y + ny - k, ny)) + large]

    def onward(s, k):
        if s < half - 1 or (s == half - 1 and k in ahead):
            go(piece(-s, k), f_send.at[s, k], f_recv.at[s, k], up)

    def backward(s, k):
        if s < half - 1 or (s == half - 1 and k not in ahead):
            go(piece(s, k), b_send.at[s, k], b_recv.at[s, k], down)

    def relay(s, k):
        if s == 0:
            if k:
                who = peer(z, lax.rem(y + ny - k, ny), c)
                arrived(piece(0, k), y_send.at[k], y_recv.at[k], who)
            onward(s, k)
            backward(s, k)
        else:
            if s < half or k in ahead:
                arrived(piece(-s, k), f_send.at[s - 1, k], f_recv.at[s - 1, k], down)
                onward(s, k)
            if s < half or k not in ahead:
                arrived(piece(s, k), b_send.at[s - 1, k], b_recv.at[s - 1, k], up)
                backward(s, k)

    for k in near_y:
        relay(0, k)
    for d in reversed(far_z):
        zz = lax.rem(z + nz - d, nz)
        arrived(g_ref.at[(zz, y) + small], sz_send.at[d], sz_recv.at[d], peer(zz, y, c))
    for d in far_y:
        ref = g_ref.at[(slice(None), y) + small]
        go(ref, sy_send.at[d], sy_recv.at[d], peer(z, lax.rem(y + d, ny), c))
    for s in range(1, half + 1):
        for k in near_y:
            relay(s, k)
    for d in reversed(far_y):
        yy = lax.rem(y + ny - d, ny)
        ref = g_ref.at[(slice(None), yy) + small]
        arrived(ref, sy_send.at[d], sy_recv.at[d], peer(z, yy, c))
    return pending


def ctx_peer(ny):
    return lambda z, y, c: {"ctx": (z * ny + y) * 2 + c}


def ring_peers(nz, ny, at, peer):
    z, y, c = at
    out = [peer(z, lax.rem(y + d, ny), c) for d in range(1, ny)]
    return out + [peer(lax.rem(z + d, nz), y, c) for d in range(1, nz)]


def swap_tokens(nz, ny, inputs, q_buf, kv_buf, weights, send, recv, own):
    z, y, c = place(ny)
    other = ctx_peer(ny)(z, y, 1 - c)
    mine = pl.ds(pl.multiple_of(c * HD, HD), HD)
    theirs = pl.ds(pl.multiple_of((1 - c) * HD, HD), HD)
    spots = [
        lambda t: q_buf.at[t],
        lambda t: kv_buf.at[z, y, t, :, pl.ds(0, HD)],
        lambda t: kv_buf.at[z, y, t, :, pl.ds(HD, HD)],
    ]
    sent, kept = [], []
    for i, (x, spot) in enumerate(zip(inputs, spots)):
        copy = remote(x.at[:, theirs], spot(c), send.at[i], recv.at[i], other)
        copy.start()
        sent.append(copy)
        copy = pltpu.make_async_copy(x.at[:, mine], spot(c), own.at[i])
        copy.start()
        kept.append(copy)
    for copy in kept:
        copy.wait()
    for i, spot in enumerate(spots):
        got = spot(1 - c)
        remote(got, got, send.at[i], recv.at[i], other).wait_recv()
    swaps = [
        remote(src, dst, send.at[3 + i], recv.at[3 + i], other) for i, (src, dst) in enumerate(weights)
    ]
    for copy in swaps:
        copy.start()
    return sent, swaps


def attend(nz, q_buf, kv_buf, mask_ref, s_buf, a_buf):
    tokens = q_buf.shape[0] * q_buf.shape[1]
    queries = q_buf[...].reshape(tokens, HD)
    span = s_buf.shape[1] // nz
    top = jnp.full((tokens, 1), -1e30, jnp.float32)
    for i in range(nz):
        cols = slice(i * span, (i + 1) * span)
        keys = kv_buf[i, :, :, :, :HD].reshape(span, HD)
        scores = lax.dot_general(
            queries, keys, (((1,), (1,)), ((), ())), preferred_element_type=jnp.float32
        ) * (1.0 / math.sqrt(HD))
        scores = jnp.where(mask_ref[:, cols] > 0, scores, -1e30)
        s_buf[:, cols] = scores
        top = jnp.maximum(top, jnp.max(scores, axis=1, keepdims=True))
    total = jnp.zeros((tokens, 1), jnp.float32)
    product = jnp.zeros((tokens, HD), jnp.float32)
    for i in range(nz):
        cols = slice(i * span, (i + 1) * span)
        values = kv_buf[i, :, :, :, HD:].reshape(span, HD)
        expo = jnp.where(mask_ref[:, cols] > 0, jnp.exp(s_buf[:, cols] - top), 0.0)
        total = total + jnp.sum(expo, axis=1, keepdims=True)
        product = product + jnp.dot(
            expo.astype(jnp.bfloat16), values, preferred_element_type=jnp.float32
        )
    a_buf[...] = (product / total).astype(jnp.bfloat16).reshape(a_buf.shape)


def ring_sems(nz, ny):
    return [DMA((ny,))] * 2 + [DMA((nz // 2, ny))] * 4 + [DMA((nz,))] * 2 + [DMA((ny,))] * 2


def swap_heads(ny, ne, a_ref, o_ref, own, send, recv):
    z, y, c = place(ny)
    e = lax.axis_index("exp")
    keep = pltpu.make_async_copy(a_ref.at[c], o_ref.at[e, c], own)
    keep.start()
    others = [(de, dc) for de in range(ne) for dc in range(2) if de or dc]
    copies = []
    for de, dc in others:
        to = {"ctx": (z * ny + y) * 2 + lax.rem(c + dc, 2), "exp": lax.rem(e + de, ne)}
        copy = remote(a_ref.at[lax.rem(c + dc, 2)], o_ref.at[e, c], send.at[de, dc], recv.at[de, dc], to)
        copy.start()
        copies.append(copy)
    keep.wait()
    for de, dc in others:
        back = lax.rem(e + ne - de, ne)
        got = o_ref.at[back, lax.rem(c + dc, 2)]
        remote(got, got, send.at[de, dc], recv.at[de, dc], {"exp": back}).wait_recv()
    return copies


def swap_pieces(ne, x_ref, o_ref, own, send, recv):
    e = lax.axis_index("exp")
    keep = pltpu.make_async_copy(x_ref.at[e], o_ref.at[e], own)
    keep.start()
    copies = []
    for de in range(1, ne):
        to = lax.rem(e + de, ne)
        copy = remote(x_ref.at[to], o_ref.at[e], send.at[de], recv.at[de], {"exp": to})
        copy.start()
        copies.append(copy)
    keep.wait()
    for de in range(1, ne):
        back = lax.rem(e + ne - de, ne)
        got = o_ref.at[back]
        remote(got, got, send.at[de], recv.at[de], {"exp": back}).wait_recv()
    return copies


def sum_rows(nz, ny, t_ref, own_rows, o_ref, rz, ry, uz, uy, vz, vy, sems):
    z, y, c = place(ny)
    rz_send, rz_recv, ry_send, ry_recv, vz_send, vz_recv, vy_send, vy_recv = sems
    half = t_ref.shape[-1] // 2
    left, right = pl.ds(0, half), pl.ds(half, half)
    peer = ctx_peer(ny)
    far_z = sorted(range(1, nz), key=lambda d: -min(d, nz - d))
    far_y = sorted(range(1, ny), key=lambda d: -min(d, ny - d))
    to_z = {d: lax.rem(z + d, nz) for d in far_z}
    to_y = {d: lax.rem(y + d, ny) for d in far_y}

    def send(src, dst, sends, recvs, who):
        copy = remote(src, dst, sends, recvs, who)
        copy.start()
        return copy

    by_z = [
        send(t_ref.at[to_z[d], :, :, left], rz.at[d], rz_send.at[d], rz_recv.at[d], peer(to_z[d], y, c))
        for d in far_z
    ]
    by_y = [
        send(t_ref.at[:, to_y[d], :, right], ry.at[d], ry_send.at[d], ry_recv.at[d], peer(z, to_y[d], c))
        for d in far_y
    ]
    total = t_ref[z, :, :, :half].astype(jnp.float32)
    for d, copy in zip(far_z, by_z):
        copy.wait_recv()
        total = total + rz[d].astype(jnp.float32)
    uz[...] = total.astype(jnp.bfloat16)
    then_y = [
        send(uz.at[to_y[d]], vz.at[d], vz_send.at[d], vz_recv.at[d], peer(z, to_y[d], c)) for d in far_y
    ]
    total = t_ref[:, y, :, half:].astype(jnp.float32)
    for d, copy in zip(far_y, by_y):
        copy.wait_recv()
        total = total + ry[d].astype(jnp.float32)
    uy[...] = total.astype(jnp.bfloat16)
    then_z = [
        send(uy.at[to_z[d]], vy.at[d], vy_send.at[d], vy_recv.at[d], peer(to_z[d], y, c)) for d in far_z
    ]
    result = own_rows[:, :half] + uz[y].astype(jnp.float32)
    for d, copy in zip(far_y, then_y):
        copy.wait_recv()
        result = result + vz[d].astype(jnp.float32)
    o_ref[:, :half] = result.astype(jnp.bfloat16)
    result = own_rows[:, half:] + uy[z].astype(jnp.float32)
    for d, copy in zip(far_z, then_z):
        copy.wait_recv()
        result = result + vy[d].astype(jnp.float32)
    o_ref[:, half:] = result.astype(jnp.bfloat16)
    return by_z + by_y + then_y + then_z


def layer_kernel(
    nz, ny, ne, q_ref, k_ref, v_ref, mask_ref, res_ref, proj_ref, place_ref, gain_ref, w0, w1, w2,
    o_ref, q_buf, kv_buf, s_buf, a_buf, heads, pieces, own, g_buf, rows_buf, t_buf, b0, b1, b2, c0, c1, c2,
    rz, ry, uz, uy, vz, vy, local, t_send, t_recv, h_send, h_recv, p_send, p_recv, *sems
):
    at = z, y, c = place(ny)
    e = lax.axis_index("exp")
    peer = ctx_peer(ny)
    loads = [
        pltpu.make_async_copy(src, dst, local.at[2 + i])
        for i, (src, dst) in enumerate(
            [(w0, b0), (w1, b1), (w2, b2)]
        )
    ]
    for copy in loads:
        copy.start()
    greet(
        ring_peers(nz, ny, at, peer)
        + [
            {"ctx": (z * ny + y) * 2 + lax.rem(c + dc, 2), "exp": lax.rem(e + de, ne)}
            for de in range(ne)
            for dc in range(2)
            if de or dc
        ]
    )
    sent, swaps = swap_tokens(
        nz, ny, (q_ref, k_ref, v_ref), q_buf, kv_buf, [(w0, c0), (w1, c1), (w2, c2)],
        t_send, t_recv, local.at[pl.ds(5, 3)],
    )
    cut = kv_buf.shape[3] * 3 // 4
    large = (slice(None), pl.ds(0, cut))
    small = (slice(None), pl.ds(cut, kv_buf.shape[3] - cut))
    sent += spread(nz, ny, at, peer, kv_buf, large, small, sems[:10])
    attend(nz, q_buf, kv_buf, mask_ref, s_buf, a_buf)
    sent += swap_heads(ny, ne, a_buf, heads, local.at[0], h_send, h_recv)
    hidden = res_ref[...].astype(jnp.float32)
    for i in range(ne):
        for j in range(2):
            h = 2 * i + j
            hidden = hidden + jnp.dot(
                heads[i, j], proj_ref[h * HD : (h + 1) * HD, :], preferred_element_type=jnp.float32
            )
    hidden = hidden.astype(jnp.bfloat16)
    slots = jnp.dot(place_ref[...], hidden, preferred_element_type=jnp.float32)
    pieces[...] = slots.reshape(pieces.shape).astype(jnp.bfloat16)
    sent += swap_pieces(ne, pieces, own, local.at[1], p_send, p_recv)
    part = own.shape[2]
    width = ne * part
    own_f = [own[i].astype(jnp.float32) for i in range(ne)]
    square = own_f[0] * own_f[0]
    for v in own_f[1:]:
        square = square + v * v
    inv = lax.rsqrt(jnp.sum(square, axis=1, keepdims=True) / width + 1e-05)
    for i, v in enumerate(own_f):
        cols = slice(i * part, (i + 1) * part)
        g_buf[z, y, :, cols] = (v * inv * gain_ref[:, cols]).astype(jnp.bfloat16)
    cut = width * 3 // 4
    large = (slice(None), pl.ds(0, cut))
    small = (slice(None), pl.ds(cut, width - cut))
    sent += spread(nz, ny, at, peer, g_buf, large, small, sems[10:20])
    count = rows_buf.shape[0]
    rows_buf[...] = g_buf[...].astype(jnp.float32).reshape(count, width).astype(jnp.bfloat16)
    for copy in loads + swaps:
        copy.wait()
    rows = rows_buf[...]
    acts = []
    for gate, up in ((b0, b1), (c0, c1)):
        gate_v = jnp.dot(rows, gate[...], preferred_element_type=jnp.float32)
        up_v = jnp.dot(rows, up[...], preferred_element_type=jnp.float32)
        acts.append((gate_v / (1.0 + jnp.exp(-gate_v)) * up_v).astype(jnp.bfloat16))
    step = width // 4
    for i in range(4):
        cols = slice(i * step, (i + 1) * step)
        terms = jnp.dot(acts[0], b2[:, cols], preferred_element_type=jnp.float32)
        terms = terms + jnp.dot(acts[1], c2[:, cols], preferred_element_type=jnp.float32)
        t_buf[:, :, :, cols] = terms.reshape(t_buf.shape[:3] + (step,)).astype(jnp.bfloat16)
    own_rows = jnp.concatenate([own[i].astype(jnp.float32) for i in range(ne)], axis=1)
    sent += sum_rows(nz, ny, t_buf, own_rows, o_ref, rz, ry, uz, uy, vz, vy, sems[20:])
    for copy in sent:
        copy.wait_send()


def layer(
    queries, keys, values, mask, residual, out_proj, placing, gain, mine, nz, ny, ne
):
    tokens, part = residual.shape
    rows, width = tokens // ne, ne * part
    half = width // 2
    units = mine[0].shape[1]

    def buf(*shape):
        return pltpu.VMEM(shape, jnp.bfloat16)

    weights = [buf(width, units), buf(width, units), buf(units, width)]
    return pl.pallas_call(
        functools.partial(layer_kernel, nz, ny, ne),
        out_shape=jax.ShapeDtypeStruct((rows, width), jnp.bfloat16),
        in_specs=[VM] * 8 + [ANY] * 3,
        out_specs=VM,
        scratch_shapes=[
            buf(2, tokens, HD),
            buf(nz, ny, 2, tokens, 2 * HD),
            pltpu.VMEM((2 * tokens, mask.shape[1]), jnp.float32),
            buf(2, tokens, HD),
            buf(ne, 2, tokens, HD),
            buf(ne, rows, part),
            buf(ne, rows, part),
            buf(nz, ny, rows, width),
            buf(nz * ny * rows, width),
            buf(nz, ny, rows, width),
            *weights,
            *weights,
            buf(nz, ny, rows, half),
            buf(ny, nz, rows, half),
            buf(ny, rows, half),
            buf(nz, rows, half),
            buf(ny, rows, half),
            buf(nz, rows, half),
            DMA((8,)),
            DMA((6,)),
            DMA((6,)),
            DMA((ne, 2)),
            DMA((ne, 2)),
            DMA((ne,)),
            DMA((ne,)),
            *ring_sems(nz, ny),
            *ring_sems(nz, ny),
            *(DMA((n,)) for n in (nz, nz, ny, ny, ny, ny, nz, nz)),
        ],
        compiler_params=pltpu.CompilerParams(collective_id=0, has_side_effects=True),
    )(queries, keys, values, mask, residual, out_proj, placing, gain, *mine)


def body(
    residual, queries, keys, values, out_proj, norm_gain, w_gate, w_up, w_down, routes, block_mask
):
    local_tokens = residual.shape[0]
    expert_count = lax.axis_size("exp")
    ny = ROWS_Y
    nz = lax.axis_size("ctx") // (2 * ny)
    per_expert = local_tokens // expert_count
    chip = lax.axis_index("ctx") // 2
    assert 2 * local_tokens == BLK
    mask = jnp.repeat(lax.dynamic_slice_in_dim(block_mask, chip, 1, 0), BLK, axis=1)
    target = routes[:, 0]
    token_ids = jnp.arange(local_tokens, dtype=jnp.int32)
    earlier = (target[:, None] == target[None, :]) & (token_ids[None, :] < token_ids[:, None])
    ranking = jnp.sum(earlier.astype(jnp.int32), axis=1)
    slot_of = target * per_expert + ranking
    slot_ids = jnp.arange(expert_count * per_expert, dtype=jnp.int32)
    placing = (slot_of[None, :] == slot_ids[:, None]).astype(jnp.bfloat16)
    mine = (w_gate[0], w_up[0], w_down[0])
    return layer(
        queries, keys, values, mask, residual, out_proj, placing, norm_gain[None], mine, nz, ny,
        expert_count,
    )[None]


def solution(mesh):
    in_specs = (
        P("ctx", "exp"),
        P("ctx", "exp"),
        P("ctx", "exp"),
        P("ctx", "exp"),
        P(None, "exp"),
        P(),
        P("exp", None, "ctx"),
        P("exp", None, "ctx"),
        P("exp", "ctx", None),
        P("ctx", None),
        P(),
    )
    out_specs = P("exp", "ctx", None)
    return jax.shard_map(body, mesh=mesh, in_specs=in_specs, out_specs=out_specs, check_vma=False)
```
